256 devices in a mesh: feat: 64 (over z, x, y_hi), pair: 4 (over y_lo, core).
Axes of the slice: x: 4, y: 4 (y_hi: 2, y_lo: 2; y = y_hi * 2 + y_lo), z: 8, core: 2. Of those that a mesh axis runs over, the one named last changes fastest.
Arguments:
- resid: bfloat16 [4, 1024, 2048], P('pair'), may hold values from -6 to 6
- enc_weight: bfloat16 [4, 2048, 16384], P('pair', None, 'feat'), may hold values from -0.125 to 0.125
- enc_bias: float32 [4, 16384], P('pair', 'feat'), may hold values from -3 to 3
- active: int32 [4, 1024, 64], P('pair'), may hold values from 0 to 16383, all different within a row
- dec_weight: bfloat16 [4, 4, 16384, 2048], P('pair', None, 'feat'), may hold values from -0.75 to 0.75
- dec_bias: float32 [4, 2048], P('pair'), may hold values from -3 to 3
- target: bfloat16 [4, 1024, 2048], P('pair', 'feat'), may hold values from -6 to 6
Outputs:
- error: float32 [4, 1024, 2048], P('pair', 'feat')
- dec_grad: bfloat16 [4, 4, 16384, 2048], P('pair', None, 'feat')
The draws below stay inside these ranges and needn't reach their ends.
Inputs may be any that keep to these rules, and one draw needn't show every extreme that they name: `active`: within one layer, the 64 indices of a token are distinct; every feature number occurs somewhere in the array.
All inputs are finite; a program needn't handle non-finite values.
Results may differ from the reference program's by a relative error of at most 0.0058.
Values may be sent and summed in bfloat16 or wider, within the bound.
A program may use at most 128 MiB of HBM per device.

```python
import jax
import jax.numpy as jnp
from jax import lax

D = 2048
F = 16384
LAYERS = 4
K = 64
TOK = 1024


def block_scale(key, extent, cuts, least, top_value):
    def one(position, blocks):
        heights = jax.random.uniform(jax.random.fold_in(jax.random.fold_in(key, 6), position), (blocks,), jnp.float32, least / len(cuts), top_value / len(cuts))
        return jnp.repeat(jnp.exp(heights), extent[position] // blocks).reshape((-1,) + (1,) * (len(extent) - position - 1))

    factor_of = one(*cuts[0])
    for cut in cuts[1:]:
        factor_of = factor_of * one(*cut)
    return factor_of


def picks_of(key, rows, amount, top, lift):
    order = jax.random.permutation(jax.random.fold_in(key, 1), amount)
    favour = order
    for power in range(3):
        favour = favour * favour // amount
    favour = favour * lift // amount
    lots = jax.random.randint(jax.random.fold_in(key, 2), (rows, amount), 0, 4096) + favour
    holders = jax.random.permutation(jax.random.fold_in(key, 3), rows)[jnp.arange(amount) % rows]
    lots = jnp.where(jnp.arange(rows)[:, None] == holders[None, :], 1 << 14, lots)
    priority = lots * amount + jnp.arange(amount)
    return lax.top_k(priority.astype(jnp.int32), top)[1].astype(jnp.int32)


def scatter_about(stream_key, dims, spread, limit, split=(), dtype=jnp.bfloat16):
    drawn = jax.random.normal(stream_key, dims, jnp.float32) * spread
    if len(split) > 0:
        drawn = block_scale(stream_key, dims, split, -0.22, 0.18) * drawn
    return jnp.clip(drawn, min=-limit, max=limit).astype(dtype)


def setup_inputs(seed: int = 0) -> dict:
    keys = jax.random.split(jax.random.key(seed), 8)
    return {
        "resid": scatter_about(keys[0], (LAYERS, TOK, D), 1.0, 6.0, ((0, 4),)),
        "enc_weight": scatter_about(keys[1], (LAYERS, D, F), D ** -0.5, 0.125, ((0, 4), (2, 64))),
        "enc_bias": scatter_about(keys[2], (LAYERS, F), 0.5, 3.0, ((0, 4), (1, 64)), jnp.float32),
        "active": picks_of(keys[3], LAYERS * TOK, F, K, 32).reshape((LAYERS, TOK, K)),
        "dec_weight": scatter_about(keys[4], (LAYERS, LAYERS, F, D), K ** -0.5, 0.75, ((0, 4), (2, 64))),
        "dec_bias": scatter_about(keys[5], (LAYERS, D), 0.5, 3.0, ((0, 4),), jnp.float32),
        "target": scatter_about(keys[6], (LAYERS, TOK, D), 1.0, 6.0, ((0, 4), (1, 64))),
    }


def source_values(resid_layer, enc_layer, bias_layer, index_layer):
    columns = jnp.take(jnp.transpose(enc_layer), index_layer, axis=0)
    pre_act = jnp.einsum("td,tkd->tk", resid_layer.astype(jnp.float32), columns.astype(jnp.float32))
    pre_act = pre_act + jnp.take(bias_layer, index_layer)
    return jnp.maximum(pre_act, 0.0).astype(jnp.bfloat16)


def reference(resid, enc_weight, enc_bias, active, dec_weight, dec_bias, target):
    values = []
    for source in range(LAYERS):
        computed = source_values(resid[source], enc_weight[source], enc_bias[source], active[source])
        values.append(lax.optimization_barrier(computed).astype(jnp.float32))
    errors = []
    grad_table = []
    for dest in range(LAYERS):
        partial_value = jnp.zeros((TOK, D), jnp.float32)
        for source in range(dest + 1):
            picked = jnp.take(dec_weight[dest, source], active[source], axis=0)
            partial_value = partial_value + jnp.einsum("tk,tkd->td", values[source], picked.astype(jnp.float32))
        error_now = partial_value + dec_bias[dest][None, :] - target[dest].astype(jnp.float32)
        errors.append(error_now)
        rounded = lax.optimization_barrier(error_now.astype(jnp.bfloat16)).astype(jnp.float32)
        grad_row = []
        for source in range(LAYERS):
            if source <= dest:
                terms = values[source][:, :, None] * rounded[:, None, :]
                summed = jnp.zeros((F, D), jnp.float32).at[active[source]].add(terms)
                grad_row.append(summed.astype(jnp.bfloat16))
            else:
                grad_row.append(jnp.zeros((F, D), jnp.bfloat16))
        grad_table.append(jnp.stack(grad_row))
    return jnp.stack(errors), jnp.stack(grad_table)
```

```python
import jax
import jax.numpy as jnp
from jax import lax
from jax.experimental import pallas as pl
from jax.experimental.pallas import tpu as pltpu
from jax.sharding import PartitionSpec as P

MESH = pl.DeviceIdType.MESH
F32, BF16 = jnp.float32, jnp.bfloat16
NZ, NX, NY = 8, 4, 2
UP, DN = 0, 1


def values_kernel(active_ref, resid_ref, enc_ref, bias_ref, out_ref):
    width = enc_ref.shape[1]
    rows = resid_ref.shape[0]
    base = lax.axis_index("feat") * width
    local = active_ref[...].T - base
    word = lax.shift_right_arithmetic(local, 5)
    bit = lax.shift_left(jnp.int32(1), local & 31)
    words = [
        jnp.sum(jnp.where(word == w, bit, 0), axis=0, keepdims=True) for w in range(width // 32)
    ]
    spread = jnp.concatenate([jnp.broadcast_to(w, (32, rows)) for w in words], axis=0)
    place = lax.broadcasted_iota(jnp.int32, (width, rows), 0) & 31
    chosen = (lax.shift_right_logical(spread, place) & 1).astype(F32).T
    pre = jnp.dot(resid_ref[...], enc_ref[...], preferred_element_type=F32) + bias_ref[...]
    out_ref[...] = jnp.where(chosen > 0.5, jnp.maximum(pre, 0.0), 0.0).astype(BF16)


def values_of(active, resid, enc, bias):
    tokens, model = resid.shape
    width = enc.shape[1]
    block = 256
    return pl.pallas_call(
        values_kernel,
        grid=(tokens // block,),
        out_shape=jax.ShapeDtypeStruct((tokens, width), BF16),
        in_specs=[
            pl.BlockSpec((block, active.shape[1]), lambda i: (i, 0)),
            pl.BlockSpec((block, model), lambda i: (i, 0)),
            pl.BlockSpec((model, width), lambda i: (0, 0)),
            pl.BlockSpec((1, width), lambda i: (0, 0)),
        ],
        out_specs=pl.BlockSpec((block, width), lambda i: (i, 0)),
    )(active, resid, enc, bias)


def grad_kernel(cat_ref, err_ref, out_ref, turned):
    @pl.when(pl.program_id(0) == 0)
    def _():
        turned[...] = cat_ref[...].T

    layers, width, cols = out_ref.shape
    product = jnp.dot(turned[...], err_ref[...], preferred_element_type=F32)
    out_ref[...] = product.astype(BF16).reshape(layers, width, cols)


def grads_of(cat, err, layers):
    tokens, stacked = cat.shape
    model = err.shape[1]
    block = 256
    return pl.pallas_call(
        grad_kernel,
        grid=(model // block,),
        out_shape=jax.ShapeDtypeStruct((layers, stacked // layers, model), BF16),
        in_specs=[
            pl.BlockSpec((tokens, stacked), lambda i: (0, 0)),
            pl.BlockSpec((tokens, block), lambda i: (0, i)),
        ],
        out_specs=pl.BlockSpec((layers, stacked // layers, block), lambda i: (0, 0, i)),
        scratch_shapes=[pltpu.VMEM((stacked, tokens), BF16)],
    )(cat, err)


class Ring:
    def __init__(self, size, index, device, sends, recvs):
        self.size, self.index, self.device = size, index, device
        self.sends, self.recvs = sends, recvs
        self.far = size // 2
        self.started = []

    def at(self, offset):
        return lax.rem(self.index + offset + self.size, self.size)

    def copy(self, way, half, step, src, dst):
        toward = self.at(1 if way == UP else -1)
        return pltpu.make_async_remote_copy(
            src_ref=src,
            dst_ref=dst,
            send_sem=self.sends.at[way, half, step - 1],
            recv_sem=self.recvs.at[way, half, step - 1],
            device_id=self.device(toward),
            device_id_type=MESH,
        )

    def go(self, *what):
        copy = self.copy(*what)
        copy.start()
        self.started.append(copy)

    def drain(self):
        for copy in self.started:
            copy.wait_send()

    def reach(self, way, half):
        return self.far if way == half else self.far - 1


STREAMS = ((UP, 0), (DN, 1), (UP, 1), (DN, 0))


class Reduce(Ring):
    def __init__(self, size, index, device, sends, recvs, own, held):
        super().__init__(size, index, device, sends, recvs)
        self.own, self.held = own, held

    def slot(self, way, half, step):
        return self.held.at[way, half, step - 1]

    def first(self):
        for way, half in STREAMS:
            far = self.reach(way, half)
            dest = self.at(far if way == UP else -far)
            self.go(way, half, far, self.own(dest, half), self.slot(way, half, far))

    def arrive(self, way, half, step):
        slot = self.slot(way, half, step)
        self.copy(way, half, step, slot, slot).wait_recv()
        return slot

    def pass_on(self, way, half, step):
        slot = self.arrive(way, half, step + 1)
        dest = self.at(step if way == UP else -step)
        own = self.own(dest, half)
        slot[...] = (slot[...].astype(F32) + own[...].astype(F32)).astype(BF16)
        self.go(way, half, step, slot, self.slot(way, half, step))

    def total(self, half):
        up = self.arrive(UP, half, 1)
        down = self.arrive(DN, half, 1)
        own = self.own(self.index, half)
        return own[...].astype(F32) + (up[...].astype(F32) + down[...].astype(F32))


class Gather(Ring):
    def __init__(self, size, index, device, sends, recvs, view):
        super().__init__(size, index, device, sends, recvs)
        self.view = view

    def first(self):
        for way, half in STREAMS:
            block = self.view(self.index, half)
            self.go(way, half, 1, block, block)

    def arrive(self, way, half, step):
        block = self.view(self.at(-step if way == UP else step), half)
        self.copy(way, half, step, block, block).wait_recv()
        return block

    def pass_on(self, way, half, step):
        if step <= self.reach(way, half):
            block = self.arrive(way, half, step - 1)
            self.go(way, half, step, block, block)

    def last(self):
        for way, half in STREAMS:
            self.arrive(way, half, self.reach(way, half))


def exchange_kernel(
    vals_ref, dec_ref, bias_ref, target_ref,
    err_ref, full_ref, cat_ref,
    part, mid_a, mid_b, end_a, end_b,
    held_az, held_ax, held_bx, held_bz, held_y, last_y,
    pair_send, pair_recv,
    s_az, r_az, s_ax, r_ax, s_bx, r_bx, s_bz, r_bz,
    g_ax, h_ax, g_az, h_az, g_bz, h_bz, g_bx, h_bx,
    y_send, y_recv,
):
    feat, pair = lax.axis_index("feat"), lax.axis_index("pair")
    z, x, y = feat // (NX * NY), lax.rem(feat // NY, NX), lax.rem(feat, NY)
    width = vals_ref.shape[2]
    cut = part.shape[2] // 2
    cols_a, cols_b = pl.ds(0, cut), pl.ds(cut, cut)

    def spot(zz, xx, yy):
        return ((zz * NX + xx) * NY + yy, pair)

    along_z = lambda other: spot(other, x, y)
    along_x = lambda other: spot(z, other, y)
    across = spot(z, x, 1 - y)
    core_mate = (feat, pair + 1 - 2 * lax.rem(pair, 2))
    chip_mate = (feat, lax.rem(pair + 2, 4))

    barrier = pltpu.get_barrier_semaphore()
    greeted = (
        along_z(lax.rem(z + 1, NZ)), along_z(lax.rem(z + NZ - 1, NZ)),
        along_x(lax.rem(x + 1, NX)), along_x(lax.rem(x + NX - 1, NX)),
        across, core_mate, chip_mate,
    )
    for device in greeted:
        pl.semaphore_signal(barrier, inc=1, device_id=device, device_id_type=MESH)
    pl.semaphore_wait(barrier, len(greeted))

    pieces = pair_recv.shape[1]
    span = NZ // pieces

    def column(slot):
        return pl.ds(pl.multiple_of(slot * width, width), width)

    def piece(ref, slot, c):
        return ref.at[pl.ds(c * span, span), :, column(slot)]

    def send_piece(kind, src, slot, c, device):
        return pltpu.make_async_remote_copy(
            src_ref=src, dst_ref=piece(cat_ref, slot, c),
            send_sem=pair_send.at[kind, c], recv_sem=pair_recv.at[slot, c],
            device_id=device, device_id_type=MESH,
        )

    def await_piece(slot, c):
        block = piece(cat_ref, slot, c)
        send_piece(0, block, slot, c, core_mate).wait_recv()

    mine = lambda c: vals_ref.at[pl.ds(c * span, span)]
    low_chip, low_core = pair < 2, lax.rem(pair, 2) == 0
    relayed = lax.rem(pair, 2)

    @pl.when(low_chip)
    def _():
        for c in range(pieces):
            send_piece(0, mine(c), pair, c, chip_mate).start()

    @pl.when(low_core)
    def _():
        for c in range(pieces):
            send_piece(1, mine(c), pair, c, core_mate).start()

    for slot in range(4):

        @pl.when(pair == slot)
        def _():
            cat_ref[:, :, slot * width : (slot + 1) * width] = vals_ref[...]

        @pl.when(pair < slot)
        def _():
            cat_ref[:, :, slot * width : (slot + 1) * width] = jnp.zeros(
                (NZ, vals_ref.shape[1], width), BF16
            )

    @pl.when(jnp.logical_not(low_chip))
    def _():
        for c in range(pieces):
            await_piece(relayed, c)
            send_piece(2, piece(cat_ref, relayed, c), relayed, c, core_mate).start()
        for c in range(pieces):
            await_piece(1 - relayed, c)

    @pl.when(pair == 1)
    def _():
        for c in range(pieces):
            await_piece(0, c)

    @pl.when(pair == 3)
    def _():
        for c in range(pieces):
            await_piece(2, c)

    step = 256

    @pl.loop(0, part.shape[2] // step)
    def _(i):
        cols = pl.ds(pl.multiple_of(i * step, step), step)
        rows = cat_ref[...].reshape(-1, cat_ref.shape[2])
        product = jnp.dot(rows, dec_ref[:, cols], preferred_element_type=F32)
        part[:, :, cols] = product.astype(BF16).reshape(NZ, -1, step)

    def rows32(index, half):
        return pl.ds(pl.multiple_of(index * 32 + half * 16, 16), 16)

    az = Reduce(NZ, z, along_z, s_az, r_az, lambda i, h: part.at[i, pl.ds(h * 64, 64), cols_a], held_az)
    bx = Reduce(
        NX, x, along_x, s_bx, r_bx,
        lambda i, h: part.at[pl.ds(h * 4, 4), pl.ds(pl.multiple_of(i * 32, 32), 32), cols_b], held_bx,
    )
    ax = Reduce(NX, x, along_x, s_ax, r_ax, lambda i, h: mid_a.at[rows32(i, h)], held_ax)
    bz = Reduce(NZ, z, along_z, s_bz, r_bz, lambda i, h: mid_b.at[i, pl.ds(h * 16, 16)], held_bz)
    az.first()
    bx.first()
    az.pass_on(UP, 0, 3)
    az.pass_on(DN, 1, 3)
    az.pass_on(UP, 1, 2)
    az.pass_on(DN, 0, 2)
    bx.pass_on(UP, 0, 1)
    bx.pass_on(DN, 1, 1)
    az.pass_on(UP, 0, 2)
    az.pass_on(DN, 1, 2)
    az.pass_on(UP, 1, 1)
    az.pass_on(DN, 0, 1)
    az.pass_on(UP, 0, 1)
    az.pass_on(DN, 1, 1)
    for half in range(2):
        mid_b[half * 4 : half * 4 + 4] = bx.total(half).astype(BF16)
    bz.first()
    for half in range(2):
        mid_a[half * 64 : half * 64 + 64] = az.total(half).astype(BF16)
    ax.first()
    for way, half in ((UP, 0), (DN, 1)):
        bz.pass_on(way, half, 3)
    for way, half in ((UP, 1), (DN, 0)):
        bz.pass_on(way, half, 2)
    for way, half in ((UP, 0), (DN, 1)):
        ax.pass_on(way, half, 1)
    for way, half in ((UP, 0), (DN, 1)):
        bz.pass_on(way, half, 2)
    for way, half in ((UP, 1), (DN, 0)):
        bz.pass_on(way, half, 1)
    for way, half in ((UP, 0), (DN, 1)):
        bz.pass_on(way, half, 1)

    def over_y(which, src, dst):
        return pltpu.make_async_remote_copy(
            src_ref=src, dst_ref=dst, send_sem=y_send.at[which], recv_sem=y_recv.at[which],
            device_id=across, device_id_type=MESH,
        )

    for half in range(2):
        end_a[half] = ax.total(half)
        held_y[0, half] = end_a[half].astype(BF16)
    copy_a = over_y(0, held_y.at[0, 1 - y], last_y.at[0])
    copy_a.start()
    for half in range(2):
        end_b[half] = bz.total(half)
        held_y[1, half] = end_b[half].astype(BF16)
    copy_b = over_y(1, held_y.at[1, 1 - y], last_y.at[1])
    copy_b.start()

    my_rows = pl.ds(pl.multiple_of(x * 32 + y * 16, 16), 16)
    for which, copy, end in ((0, copy_a, end_a), (1, copy_b, end_b)):
        copy.wait_recv()
        cols = slice(which * cut, which * cut + cut)
        rebuilt = end[y] + last_y[which].astype(F32)
        error = rebuilt + bias_ref[:, cols] - target_ref[:, cols].astype(F32)
        err_ref[:, cols] = error
        full_ref[z, my_rows, cols] = error.astype(BF16)

    own_block = full_ref.at[z, my_rows]
    other_block = full_ref.at[z, pl.ds(pl.multiple_of(x * 32 + (1 - y) * 16, 16), 16)]
    copy_e = over_y(2, own_block, own_block)
    copy_e.start()
    over_y(2, other_block, other_block).wait_recv()
    gax = Gather(NX, x, along_x, g_ax, h_ax, lambda i, h: full_ref.at[z, rows32(i, h), cols_a])
    gbz = Gather(NZ, z, along_z, g_bz, h_bz, lambda i, h: full_ref.at[i, rows32(x, h), cols_b])
    gaz = Gather(NZ, z, along_z, g_az, h_az, lambda i, h: full_ref.at[i, pl.ds(h * 64, 64), cols_a])
    gbx = Gather(
        NX, x, along_x, g_bx, h_bx,
        lambda i, h: full_ref.at[pl.ds(h * 4, 4), pl.ds(pl.multiple_of(i * 32, 32), 32), cols_b],
    )
    gax.first()
    gbz.first()
    for way, half in STREAMS:
        gax.pass_on(way, half, 2)
    for way, half in STREAMS:
        gbz.pass_on(way, half, 2)
    gax.last()
    gaz.first()
    for way, half in STREAMS:
        gbz.pass_on(way, half, 3)
    for way, half in STREAMS:
        gbz.pass_on(way, half, 4)
    gbz.last()
    gbx.first()
    for way, half in STREAMS:
        gaz.pass_on(way, half, 2)
    for way, half in STREAMS:
        gbx.pass_on(way, half, 2)
    for way, half in STREAMS:
        gaz.pass_on(way, half, 3)
    for way, half in STREAMS:
        gaz.pass_on(way, half, 4)
    gbx.last()
    gaz.last()

    for ring in (az, bx, ax, bz, gax, gbz, gaz, gbx):
        ring.drain()
    for copy in (copy_a, copy_b, copy_e):
        copy.wait_send()

    @pl.when(low_chip)
    def _():
        for c in range(pieces):
            send_piece(0, mine(c), pair, c, chip_mate).wait_send()

    @pl.when(low_core)
    def _():
        for c in range(pieces):
            send_piece(1, mine(c), pair, c, core_mate).wait_send()

    @pl.when(jnp.logical_not(low_chip))
    def _():
        for c in range(pieces):
            send_piece(2, piece(cat_ref, relayed, c), relayed, c, core_mate).wait_send()


def exchange(vals, dec, bias, target):
    tokens, width = vals.shape
    stacked, model = dec.shape
    cut = model // 2
    pieces = 4
    dma = pltpu.SemaphoreType.DMA
    vmem = pl.BlockSpec(memory_space=pltpu.VMEM)
    block = tokens // NZ
    long, short = dma((2, 2, NZ // 2)), dma((2, 2, NX // 2))
    return pl.pallas_call(
        exchange_kernel,
        out_shape=(
            jax.ShapeDtypeStruct(target.shape, F32),
            jax.ShapeDtypeStruct((NZ, block, model), BF16),
            jax.ShapeDtypeStruct((NZ, block, stacked), BF16),
        ),
        in_specs=[vmem] * 4,
        out_specs=(vmem,) * 3,
        scratch_shapes=[
            pltpu.VMEM((NZ, block, model), BF16),
            pltpu.VMEM((block, cut), BF16),
            pltpu.VMEM((NZ, 32, cut), BF16),
            pltpu.VMEM((2, 16, cut), F32),
            pltpu.VMEM((2, 16, cut), F32),
            pltpu.VMEM((2, 2, NZ // 2, 64, cut), BF16),
            pltpu.VMEM((2, 2, NX // 2, 16, cut), BF16),
            pltpu.VMEM((2, 2, NX // 2, 4, 32, cut), BF16),
            pltpu.VMEM((2, 2, NZ // 2, 16, cut), BF16),
            pltpu.VMEM((2, 2, 16, cut), BF16),
            pltpu.VMEM((2, 16, cut), BF16),
            dma((3, pieces)),
            dma((4, pieces)),
            long, long, short, short, short, short, long, long,
            short, short, long, long, long, long, short, short,
            dma((3,)),
            dma((3,)),
        ],
        compiler_params=pltpu.CompilerParams(
            collective_id=0, has_side_effects=True, vmem_limit_bytes=60 * 1024 * 1024
        ),
    )(vals.reshape(NZ, block, width), dec, bias, target)


def local(resid, enc_weight, enc_bias, active, dec_weight, dec_bias, target):
    layers, width, model = dec_weight.shape[1:]
    tokens = resid.shape[1]
    vals = values_of(active[0], resid[0], enc_weight[0], enc_bias)
    error, full, cat = exchange(
        vals, dec_weight[0].reshape(layers * width, model), dec_bias, target[0]
    )
    grads = grads_of(cat.reshape(tokens, -1), full.reshape(tokens, model), layers)
    return error[None], grads[None]


def solution(mesh):
    in_specs = (
        P("pair", None, None),
        P("pair", None, "feat"),
        P("pair", "feat"),
        P("pair", None, None),
        P("pair", None, "feat", None),
        P("pair", None),
        P("pair", "feat", None),
    )
    out_specs = (P("pair", "feat", None), P("pair", None, "feat", None))
    return jax.shard_map(local, mesh=mesh, in_specs=in_specs, out_specs=out_specs, check_vma=False)
```

```python
import jax
import jax.numpy as jnp
from jax import lax
from jax.experimental import pallas as pl
from jax.experimental.pallas import tpu as pltpu
from jax.sharding import PartitionSpec as P

MESH = pl.DeviceIdType.MESH
F32, BF16 = jnp.float32, jnp.bfloat16
NZ, NX, NY = 8, 4, 2
UP, DN = 0, 1


def grad_kernel(turned_ref, err_ref, out_ref):
    layers, width, cols = out_ref.shape
    product = jnp.dot(turned_ref[...], err_ref[...], preferred_element_type=F32)
    out_ref[...] = product.astype(BF16).reshape(layers, width, cols)


def grads_of(turned, err, layers):
    stacked, tokens = turned.shape
    model = err.shape[1]
    block = 256
    return pl.pallas_call(
        grad_kernel,
        grid=(model // block,),
        out_shape=jax.ShapeDtypeStruct((layers, stacked // layers, model), BF16),
        in_specs=[
            pl.BlockSpec((stacked, tokens), lambda i: (0, 0)),
            pl.BlockSpec((tokens, block), lambda i: (0, i)),
        ],
        out_specs=pl.BlockSpec((layers, stacked // layers, block), lambda i: (0, 0, i)),
    )(turned, err)


class Ring:
    def __init__(self, size, index, device, sends, recvs):
        self.size, self.index, self.device = size, index, device
        self.sends, self.recvs = sends, recvs
        self.far = size // 2
        self.started = []

    def at(self, offset):
        return lax.rem(self.index + offset + self.size, self.size)

    def copy(self, way, half, step, src, dst):
        toward = self.at(1 if way == UP else -1)
        return pltpu.make_async_remote_copy(
            src_ref=src,
            dst_ref=dst,
            send_sem=self.sends.at[way, half, step - 1],
            recv_sem=self.recvs.at[way, half, step - 1],
            device_id=self.device(toward),
            device_id_type=MESH,
        )

    def go(self, *what):
        copy = self.copy(*what)
        copy.start()
        self.started.append(copy)

    def drain(self):
        for copy in self.started:
            copy.wait_send()

    def reach(self, way, half):
        return self.far if way == half else self.far - 1


LONG, SHORT = ((UP, 0), (DN, 1)), ((UP, 1), (DN, 0))
STREAMS = ((UP, 0), (DN, 1), (UP, 1), (DN, 0))


class Reduce(Ring):
    def __init__(self, size, index, device, sends, recvs, own, held):
        super().__init__(size, index, device, sends, recvs)
        self.own, self.held = own, held

    def slot(self, way, half, step):
        return self.held.at[way, half, step - 1]

    def first(self, streams=STREAMS):
        for way, half in streams:
            far = self.reach(way, half)
            dest = self.at(far if way == UP else -far)
            self.go(way, half, far, self.own(dest, half), self.slot(way, half, far))

    def arrive(self, way, half, step):
        slot = self.slot(way, half, step)
        self.copy(way, half, step, slot, slot).wait_recv()
        return slot

    def pass_on(self, way, half, step):
        slot = self.arrive(way, half, step + 1)
        dest = self.at(step if way == UP else -step)
        own = self.own(dest, half)
        slot[...] = (slot[...].astype(F32) + own[...].astype(F32)).astype(BF16)
        self.go(way, half, step, slot, self.slot(way, half, step))

    def both(self, streams, step):
        for way, half in streams:
            self.pass_on(way, half, step)

    def total(self, half):
        up = self.arrive(UP, half, 1)
        down = self.arrive(DN, half, 1)
        own = self.own(self.index, half)
        return own[...].astype(F32) + (up[...].astype(F32) + down[...].astype(F32))


class Gather(Ring):
    def __init__(self, size, index, device, sends, recvs, view):
        super().__init__(size, index, device, sends, recvs)
        self.view = view

    def first(self, streams=STREAMS):
        for way, half in streams:
            block = self.view(self.index, half)
            self.go(way, half, 1, block, block)

    def arrive(self, way, half, step):
        block = self.view(self.at(-step if way == UP else step), half)
        self.copy(way, half, step, block, block).wait_recv()
        return block

    def pass_on(self, way, half, step):
        if step <= self.reach(way, half):
            block = self.arrive(way, half, step - 1)
            self.go(way, half, step, block, block)

    def spread(self, step):
        for way, half in STREAMS:
            self.pass_on(way, half, step)

    def last(self, streams=STREAMS):
        for way, half in streams:
            self.arrive(way, half, self.reach(way, half))


BLOCK = 128


def step_kernel(
    act_ref, resid_hbm, enc_hbm, enc_bias_ref, dec_hbm, dec_bias_ref, target_ref,
    err_ref, full_ref, turned_ref,
    resid, enc, dec, cat, part, mid_a, mid_b, end_a, end_b,
    held_az, held_ax, held_bx, held_bz, give_a, give_b, take_a, take_b,
    load, pair_send, pair_recv,
    s_az, r_az, s_ax, r_ax, s_bx, r_bx, s_bz, r_bz,
    g_ax, h_ax, g_az, h_az, g_bz, h_bz, g_bx, h_bx,
    y_send, y_recv,
):
    feat, pair = lax.axis_index("feat"), lax.axis_index("pair")
    z, x, y = feat // (NX * NY), lax.rem(feat // NY, NX), lax.rem(feat, NY)
    width = enc.shape[1]
    cut = mid_a.shape[1]
    cols_a, cols_b = pl.ds(0, cut), pl.ds(cut, part.shape[2] - cut)

    near_z = lambda by: lax.rem(z + by + NZ, NZ)
    near_x = lambda by: lax.rem(x + by + NX, NX)
    order = [near_z(by) for by in (4, 3, -3, 2, -2, 1, -1, 0)]

    enc_copy = pltpu.make_async_copy(enc_hbm, enc, load.at[NZ])
    dec_copy = pltpu.make_async_copy(dec_hbm, dec, load.at[NZ + 1])
    resid_copies = [
        pltpu.make_async_copy(
            resid_hbm.at[pl.ds(pl.multiple_of(o * BLOCK, BLOCK), BLOCK)], resid.at[k], load.at[k]
        )
        for k, o in enumerate(order)
    ]
    enc_copy.start()
    for copy in resid_copies[:2]:
        copy.start()
    dec_copy.start()
    for copy in resid_copies[2:]:
        copy.start()

    def spot(zz, xx, yy):
        return ((zz * NX + xx) * NY + yy, pair)

    along_z = lambda other: spot(other, x, y)
    along_x = lambda other: spot(z, other, y)
    across = spot(z, x, 1 - y)
    core_mate = (feat, pair + 1 - 2 * lax.rem(pair, 2))
    chip_mate = (feat, lax.rem(pair + 2, 4))

    barrier = pltpu.get_barrier_semaphore()
    greeted = (
        along_z(near_z(1)), along_z(near_z(-1)), along_x(near_x(1)), along_x(near_x(-1)),
        across, core_mate, chip_mate,
    )
    for device in greeted:
        pl.semaphore_signal(barrier, inc=1, device_id=device, device_id_type=MESH)

    for slot in range(1, 4):

        @pl.when(pair < slot)
        def _():
            cat[:, :, slot * width : (slot + 1) * width] = jnp.zeros((NZ, BLOCK, width), BF16)

    pl.semaphore_wait(barrier, len(greeted))

    low_chip, low_core = pair < 2, lax.rem(pair, 2) == 0
    relayed = lax.rem(pair, 2)

    def piece(slot, k):
        return cat.at[order[k], :, pl.ds(pl.multiple_of(slot * width, width), width)]

    def send_piece(kind, slot, k, device):
        return pltpu.make_async_remote_copy(
            src_ref=piece(slot, k), dst_ref=piece(slot, k),
            send_sem=pair_send.at[kind, k], recv_sem=pair_recv.at[slot, k],
            device_id=device, device_id_type=MESH,
        )

    def await_piece(slot, k):
        send_piece(0, slot, k, core_mate).wait_recv()

    def values(k):
        resid_copies[k].wait()
        if k == 0:
            enc_copy.wait()
        tokens = pl.ds(pl.multiple_of(order[k] * BLOCK, BLOCK), BLOCK)
        local = act_ref[:, tokens] - feat * width
        word = lax.shift_right_arithmetic(local, 5)
        bit = lax.shift_left(jnp.int32(1), local & 31)
        words = [
            jnp.sum(jnp.where(word == w, bit, 0), axis=0, keepdims=True)
            for w in range(width // 32)
        ]
        spread = jnp.concatenate([jnp.broadcast_to(w, (32, BLOCK)) for w in words], axis=0)
        place = lax.broadcasted_iota(jnp.int32, (width, BLOCK), 0) & 31
        chosen = (lax.shift_right_logical(spread, place) & 1).astype(F32).T
        pre = jnp.dot(resid[k], enc[...], preferred_element_type=F32) + enc_bias_ref[...]
        found = jnp.where(chosen > 0.5, jnp.maximum(pre, 0.0), 0.0).astype(BF16)
        piece(pair, k)[...] = found

        @pl.when(low_chip)
        def _():
            send_piece(0, pair, k, chip_mate).start()

        @pl.when(low_core)
        def _():
            send_piece(1, pair, k, core_mate).start()

    def relay(*ks):
        @pl.when(jnp.logical_not(low_chip))
        def _():
            for k in ks:
                await_piece(relayed, k)
                send_piece(2, relayed, k, core_mate).start()

    def decode(*ks):
        if ks[0] == 0:
            dec_copy.wait()

        @pl.when(jnp.logical_not(low_chip))
        def _():
            for k in ks:
                await_piece(1 - relayed, k)

        for holder, slot in ((1, 0), (3, 2)):

            @pl.when(pair == holder)
            def _():
                for k in ks:
                    await_piece(slot, k)

        step = 512

        @pl.loop(0, part.shape[2] // step)
        def _(i):
            cols = pl.ds(pl.multiple_of(i * step, step), step)
            rows = jnp.concatenate([cat[order[k]] for k in ks], axis=0)
            product = jnp.dot(rows, dec[:, cols], preferred_element_type=F32).astype(BF16)
            for n, k in enumerate(ks):
                part[order[k], :, cols] = product[n * BLOCK : (n + 1) * BLOCK]

    def rows16(index, half):
        return pl.ds(pl.multiple_of(index * 32 + half * 16, 16), 16)

    az = Reduce(NZ, z, along_z, s_az, r_az, lambda i, h: part.at[i, pl.ds(h * 64, 64), cols_a], held_az)
    ax = Reduce(NX, x, along_x, s_ax, r_ax, lambda i, h: mid_a.at[rows16(i, h)], held_ax)
    bx = [
        Reduce(
            NX, x, along_x, s_bx.at[k], r_bx.at[k],
            lambda i, h, o=o: part.at[o, rows16(i, h), cols_b], held_bx.at[k],
        )
        for k, o in enumerate(order)
    ]
    bz = Reduce(NZ, z, along_z, s_bz, r_bz, lambda i, h: mid_b.at[i, pl.ds(h * 16, 16)], held_bz)

    def settle(*ks):
        for k in ks:
            for half in range(2):
                mid_b[order[k], half * 16 : half * 16 + 16] = bx[k].total(half).astype(BF16)

    for k in range(3):
        values(k)
    relay(0)
    values(3)
    values(4)
    relay(1, 2)
    decode(0)
    az.first(LONG)
    bx[0].first()
    values(5)
    values(6)
    relay(3, 4)
    decode(1, 2)
    az.first(SHORT)
    bx[1].first()
    bx[2].first()
    values(7)
    relay(5, 6)
    az.both(LONG, 3)
    decode(3, 4)
    bx[3].first()
    bx[4].first()
    bx[0].both(LONG, 1)
    relay(7)
    az.both(SHORT, 2)
    decode(5, 6)
    bx[5].first()
    bx[6].first()
    bx[1].both(LONG, 1)
    bx[2].both(LONG, 1)
    az.both(LONG, 2)
    decode(7)
    bx[7].first()
    settle(0)
    bz.first(LONG)
    bx[3].both(LONG, 1)
    bx[4].both(LONG, 1)
    az.both(SHORT, 1)
    settle(1, 2)
    bz.first(SHORT)
    bz.both(LONG, 3)
    bx[5].both(LONG, 1)
    bx[6].both(LONG, 1)
    az.both(LONG, 1)
    bx[7].both(LONG, 1)
    settle(3, 4)
    bz.both(SHORT, 2)
    bz.both(LONG, 2)
    settle(5, 6)
    bz.both(SHORT, 1)
    for half in range(2):
        mid_a[half * 64 : half * 64 + 64] = az.total(half).astype(BF16)
    ax.first()
    bz.both(LONG, 1)
    settle(7)
    ax.both(LONG, 1)

    def over_y(which, src, dst):
        return pltpu.make_async_remote_copy(
            src_ref=src, dst_ref=dst, send_sem=y_send.at[which], recv_sem=y_recv.at[which],
            device_id=across, device_id_type=MESH,
        )

    last_copies = []
    for which, ring, end, give, take in ((0, ax, end_a, give_a, take_a), (1, bz, end_b, give_b, take_b)):
        for half in range(2):
            end[half] = ring.total(half)
            give[half] = end[half].astype(BF16)
        copy = over_y(which, give.at[1 - y], take)
        copy.start()
        last_copies.append(copy)

    def rows_of(xx, half):
        return rows16(xx, y if half == 0 else 1 - y)

    gax = Gather(NX, x, along_x, g_ax, h_ax, lambda i, h: full_ref.at[z, rows_of(i, h), cols_a])
    gbz = Gather(NZ, z, along_z, g_bz, h_bz, lambda i, h: full_ref.at[i, rows_of(x, h), cols_b])
    gaz = {
        by: Gather(
            NZ, z, along_z, g_az.at[n], h_az.at[n],
            lambda i, h, xx=near_x(by): full_ref.at[i, rows_of(xx, h), cols_a],
        )
        for n, by in enumerate((0, -1, 1, 2))
    }
    gbx = {
        by: Gather(
            NX, x, along_x, g_bx.at[n], h_bx.at[n],
            lambda i, h, zz=near_z(by): full_ref.at[zz, rows_of(i, h), cols_b],
        )
        for n, by in enumerate((0, -1, 1, -2, 2, -3, 3, 4))
    }
    mine, theirs = ((UP, 0), (DN, 0)), ((UP, 1), (DN, 1))
    y_copies = []
    for which, end, take, first, then in ((0, end_a, take_a, gax, gaz), (1, end_b, take_b, gbz, gbx)):
        last_copies[which].wait_recv()
        cols = slice(0, cut) if which == 0 else slice(cut, part.shape[2])
        error = end[y] + take[...].astype(F32) + dec_bias_ref[:, cols] - target_ref[:, cols].astype(F32)
        full_ref[z, rows_of(x, 0), cols] = error.astype(BF16)
        block = full_ref.at[z, rows_of(x, 0), cols]
        copy = over_y(2 + which, block, block)
        copy.start()
        y_copies.append(copy)
        first.first(mine)
        then[0].first(mine)
        err_ref[:, cols] = error
    for which, first, then in ((0, gax, gaz), (1, gbz, gbx)):
        cols = cols_a if which == 0 else cols_b
        block = full_ref.at[z, rows_of(x, 1), cols]
        over_y(2 + which, block, block).wait_recv()
        first.first(theirs)
        then[0].first(theirs)

    gax.pass_on(UP, 0, 2)
    gax.last(((UP, 1),))
    gaz[-1].first()
    gax.pass_on(DN, 1, 2)
    gax.last(((DN, 0),))
    gaz[1].first()
    gbz.spread(2)
    gbx[-1].first()
    gbx[1].first()
    gaz[0].spread(2)
    gax.last(LONG)
    gaz[2].first()
    gbx[0].spread(2)
    gbz.spread(3)
    gbx[-2].first()
    gbx[2].first()
    for n in range(4):
        tokens = pl.ds(n * 256, 256)
        turned_ref[:, tokens] = cat[2 * n : 2 * n + 2].reshape(256, -1).T
        if n == 0:
            gaz[-1].spread(2)
            gaz[1].spread(2)
            gbx[-1].spread(2)
            gbx[1].spread(2)
        if n == 1:
            gbz.spread(4)
            gbz.last(SHORT)
            gbx[-3].first()
            gbx[3].first()
            gaz[0].spread(3)
        if n == 2:
            gaz[2].spread(2)
            gbz.last(LONG)
            gbx[4].first()
            gaz[-1].spread(3)
            gaz[1].spread(3)
    gbx[-2].spread(2)
    gbx[2].spread(2)
    gaz[0].spread(4)
    gaz[2].spread(3)
    gbx[-3].spread(2)
    gbx[3].spread(2)
    gaz[-1].spread(4)
    gaz[1].spread(4)
    gbx[4].spread(2)
    gaz[2].spread(4)
    for by in (0, -1, 1, -2, 2, -3, 3, 4):
        gbx[by].last()
    for by in (0, -1, 1, 2):
        gaz[by].last()

    for ring in (az, ax, bz, *bx, gax, gbz, *gaz.values(), *gbx.values()):
        ring.drain()
    for copy in last_copies + y_copies:
        copy.wait_send()

    @pl.when(low_chip)
    def _():
        for k in range(NZ):
            send_piece(0, pair, k, chip_mate).wait_send()

    @pl.when(low_core)
    def _():
        for k in range(NZ):
            send_piece(1, pair, k, core_mate).wait_send()

    @pl.when(jnp.logical_not(low_chip))
    def _():
        for k in range(NZ):
            send_piece(2, relayed, k, core_mate).wait_send()


def step(active, resid, enc, enc_bias, dec, dec_bias, target):
    tokens, model = resid.shape
    width, stacked = enc.shape[1], dec.shape[0]
    cut = 896
    rest = model - cut
    dma, vmem = pltpu.SemaphoreType.DMA, pltpu.VMEM
    here, there = pl.BlockSpec(memory_space=pltpu.VMEM), pl.BlockSpec(memory_space=pl.ANY)
    long, short = (2, 2, NZ // 2), (2, 2, NX // 2)
    return pl.pallas_call(
        step_kernel,
        out_shape=(
            jax.ShapeDtypeStruct(target.shape, F32),
            jax.ShapeDtypeStruct((NZ, BLOCK, model), BF16),
            jax.ShapeDtypeStruct((stacked, tokens), BF16),
        ),
        in_specs=[here, there, there, here, there, here, here],
        out_specs=(here,) * 3,
        scratch_shapes=[
            vmem((NZ, BLOCK, model), BF16),
            vmem((model, width), BF16),
            vmem((stacked, model), BF16),
            vmem((NZ, BLOCK, stacked), BF16),
            vmem((NZ, BLOCK, model), BF16),
            vmem((BLOCK, cut), BF16),
            vmem((NZ, 32, rest), BF16),
            vmem((2, 16, cut), F32),
            vmem((2, 16, rest), F32),
            vmem((*long, 64, cut), BF16),
            vmem((*short, 16, cut), BF16),
            vmem((NZ, *short, 16, rest), BF16),
            vmem((*long, 16, rest), BF16),
            vmem((2, 16, cut), BF16),
            vmem((2, 16, rest), BF16),
            vmem((16, cut), BF16),
            vmem((16, rest), BF16),
            dma((NZ + 2,)),
            dma((3, NZ)),
            dma((4, NZ)),
            dma(long), dma(long), dma(short), dma(short),
            dma((NZ, *short)), dma((NZ, *short)), dma(long), dma(long),
            dma(short), dma(short), dma((4, *long)), dma((4, *long)),
            dma(long), dma(long), dma((NZ, *short)), dma((NZ, *short)),
            dma((4,)),
            dma((4,)),
        ],
        compiler_params=pltpu.CompilerParams(
            collective_id=0, has_side_effects=True, vmem_limit_bytes=60 * 1024 * 1024
        ),
    )(active, resid, enc, enc_bias, dec, dec_bias, target)


def local(resid, enc_weight, enc_bias, active, dec_weight, dec_bias, target):
    layers, width, model = dec_weight.shape[1:]
    tokens = resid.shape[1]
    error, full, turned = step(
        active[0].T, resid[0], enc_weight[0], enc_bias,
        dec_weight[0].reshape(layers * width, model), dec_bias, target[0],
    )
    grads = grads_of(turned, full.reshape(tokens, model), layers)
    return error[None], grads[None]


def solution(mesh):
    in_specs = (
        P("pair", None, None),
        P("pair", None, "feat"),
        P("pair", "feat"),
        P("pair", None, None),
        P("pair", None, "feat", None),
        P("pair", None),
        P("pair", "feat", None),
    )
    out_specs = (P("pair", "feat", None), P("pair", None, "feat", None))
    return jax.shard_map(local, mesh=mesh, in_specs=in_specs, out_specs=out_specs, check_vma=False)
```

```python
import jax
import jax.numpy as jnp
from jax import lax
from jax.experimental import pallas as pl
from jax.experimental.pallas import tpu as pltpu
from jax.sharding import PartitionSpec as P

MESH = pl.DeviceIdType.MESH
F32, BF16 = jnp.float32, jnp.bfloat16
NZ, NX, NY = 8, 4, 2
UP, DN = 0, 1


BLOCK = 128
SETS = ((384, 640), (512, 512))
GROUPS = ((0,), (1, 2), (3, 4), (5, 6), (7,))
DISTANCES = (4, 3, -3, 2, -2, 1, -1, 0)
LONG, SHORT = ((UP, 0), (DN, 1)), ((UP, 1), (DN, 0))
STREAMS = LONG + SHORT
WIRE, LATENCY = 47e3, 1.9


class Plan:
    def __init__(self):
        self.steps, self.sender = [], {}

    def add(self, run, took, after=(), needs=(), sends=(), bias=0.0):
        me = len(self.steps)
        self.steps.append((run, took, tuple(after), tuple(needs), tuple(sends), bias))
        for key, _, _ in sends:
            self.sender[key] = me
        return me

    def order(self):
        count = len(self.steps)
        follows = [[] for _ in range(count)]
        ahead = [0] * count
        size = {key: n for step in self.steps for key, _, n in step[4]}
        for me, (_, _, after, needs, _, _) in enumerate(self.steps):
            for other in after:
                follows[other].append((me, 0.0))
            for key in needs:
                follows[self.sender[key]].append((me, LATENCY + size[key] / WIRE))
            ahead[me] = len(after) + len(needs)
        level, left = [0.0] * count, ahead[:]
        queue = [me for me in range(count) if left[me] == 0]
        for me in queue:
            for other, _ in follows[me]:
                left[other] -= 1
                if left[other] == 0:
                    queue.append(other)
        for me in reversed(queue):
            level[me] = self.steps[me][1] + max((d + level[o] for o, d in follows[me]), default=0.0)
        now, free, landed, done, result = 0.0, {}, {}, [False] * count, []
        waiting = list(range(count))
        while waiting:
            best = None
            for me in waiting:
                _, _, after, needs, _, bias = self.steps[me]
                if all(done[o] for o in after) and all(key in landed for key in needs):
                    at = max([now] + [landed[key] for key in needs])
                    rank = (at > now, at if at > now else 0.0, -level[me] - bias, me)
                    if best is None or rank < best[0]:
                        best = (rank, me, at)
            _, me, at = best
            now = at + self.steps[me][1]
            for key, link, n in self.steps[me][4]:
                start = max(now, free.get(link, 0.0))
                free[link] = start + n / WIRE
                landed[key] = free[link] + LATENCY
            done[me] = True
            waiting.remove(me)
            result.append(me)
        self.length = now
        return result

    def run(self):
        for me in self.order():
            self.steps[me][0]()


class Ring:
    def __init__(self, name, size, index, device, link, nbytes, sends, recvs):
        self.name, self.size, self.index, self.device = name, size, index, device
        self.link, self.nbytes, self.sends, self.recvs = link, nbytes, sends, recvs
        self.far = size // 2
        self.started = []

    def at(self, offset):
        return lax.rem(self.index + offset + self.size, self.size)

    def copy(self, way, half, step, src, dst):
        toward = self.at(1 if way == UP else -1)
        return pltpu.make_async_remote_copy(
            src_ref=src,
            dst_ref=dst,
            send_sem=self.sends.at[way, half, step - 1],
            recv_sem=self.recvs.at[way, half, step - 1],
            device_id=self.device(toward),
            device_id_type=MESH,
        )

    def go(self, *what):
        copy = self.copy(*what)
        copy.start()
        self.started.append(copy)

    def drain(self):
        for copy in self.started:
            copy.wait_send()

    def reach(self, way, half):
        return self.far if way == half else self.far - 1

    def key(self, way, half, step):
        return (*self.name, way, half, step)

    def message(self, way, half, step):
        return (self.key(way, half, step), self.link + str(way), self.nbytes)


class Reduce(Ring):
    def __init__(self, *ring, own, held):
        super().__init__(*ring)
        self.own, self.held = own, held

    def slot(self, way, half, step):
        return self.held.at[way, half, step - 1]

    def first(self, way, half):
        far = self.reach(way, half)
        dest = self.at(far if way == UP else -far)
        self.go(way, half, far, self.own(dest, half), self.slot(way, half, far))

    def arrive(self, way, half, step):
        slot = self.slot(way, half, step)
        self.copy(way, half, step, slot, slot).wait_recv()
        return slot

    def pass_on(self, way, half, step):
        slot = self.arrive(way, half, step + 1)
        own = self.own(self.at(step if way == UP else -step), half)
        slot[...] = (slot[...].astype(F32) + own[...].astype(F32)).astype(BF16)
        self.go(way, half, step, slot, self.slot(way, half, step))

    def total(self, half):
        up = self.arrive(UP, half, 1)
        down = self.arrive(DN, half, 1)
        own = self.own(self.index, half)
        return own[...].astype(F32) + (up[...].astype(F32) + down[...].astype(F32))

    def plan(self, plan, ready, finish, took, bias):
        for way, half in STREAMS:
            sign = 1 if way == UP else -1
            far = self.reach(way, half)
            plan.add(
                lambda w=way, h=half: self.first(w, h), 0.04,
                after=ready(sign * far, half), sends=[self.message(way, half, far)], bias=bias,
            )
            for step in range(far - 1, 0, -1):
                plan.add(
                    lambda w=way, h=half, s=step: self.pass_on(w, h, s), took,
                    after=ready(sign * step, half), needs=[self.key(way, half, step + 1)],
                    sends=[self.message(way, half, step)], bias=bias,
                )
        return [
            plan.add(
                lambda h=half: finish(h, self.total(h)), 1.5 * took,
                after=ready(0, half), needs=[self.key(way, half, 1) for way in (UP, DN)], bias=bias,
            )
            for half in range(2)
        ]


class Gather(Ring):
    def __init__(self, *ring, view):
        super().__init__(*ring)
        self.view = view

    def first(self, half):
        for way in (UP, DN):
            block = self.view(self.index, half)
            self.go(way, half, 1, block, block)

    def first_messages(self, half):
        return [self.message(way, half, 1) for way in (UP, DN)]

    def arrive(self, way, half, step):
        block = self.view(self.at(-step if way == UP else step), half)
        self.copy(way, half, step, block, block).wait_recv()
        if step < self.reach(way, half):
            self.go(way, half, step + 1, block, block)

    def plan(self, plan, then=None):
        added = []
        for way, half in STREAMS:
            for step in range(1, self.reach(way, half) + 1):
                sends = [self.message(way, half, step + 1)] if step < self.reach(way, half) else []
                ring = then(-step if way == UP else step) if then else None
                if ring:
                    sends += ring.first_messages(half)

                def run(w=way, h=half, s=step, ring=ring):
                    self.arrive(w, h, s)
                    if ring:
                        ring.first(h)

                added.append(plan.add(run, 0.06 + 0.03 * len(sends), needs=[self.key(way, half, step)], sends=sends))
        return added


def step_kernel(
    act_ref, resid_hbm, enc_hbm, enc_bias_ref, dec_hbm, dec_bias_ref, target_ref,
    err_ref, grads_hbm,
    resid, enc, dec, cat, part, full, turned, grads,
    mid_a, mid_b, end, give, take, held_az, held_ax, held_bx, held_bz,
    load, store, pair_send, pair_recv,
    s_az, r_az, s_ax, r_ax, s_bx, r_bx, s_bz, r_bz,
    g_ax, h_ax, g_az, h_az, g_bz, h_bz, g_bx, h_bx,
    y_send, y_recv,
):
    feat, pair = lax.axis_index("feat"), lax.axis_index("pair")
    z, x, y = feat // (NX * NY), lax.rem(feat // NY, NX), lax.rem(feat, NY)
    width = enc.shape[1]

    near_z = lambda by: lax.rem(z + by + NZ, NZ)
    near_x = lambda by: lax.rem(x + by + NX, NX)
    order = [near_z(by) for by in DISTANCES]
    place_of = {by: k for k, by in enumerate(DISTANCES)}

    enc_copy = pltpu.make_async_copy(enc_hbm, enc, load.at[NZ])
    dec_copy = pltpu.make_async_copy(dec_hbm, dec, load.at[NZ + 1])
    resid_copies = [
        pltpu.make_async_copy(
            resid_hbm.at[pl.ds(pl.multiple_of(o * BLOCK, BLOCK), BLOCK)], resid.at[k], load.at[k]
        )
        for k, o in enumerate(order)
    ]
    enc_copy.start()
    for copy in resid_copies[:3]:
        copy.start()
    dec_copy.start()
    for copy in resid_copies[3:]:
        copy.start()

    def spot(zz, xx, yy):
        return ((zz * NX + xx) * NY + yy, pair)

    along_z = lambda other: spot(other, x, y)
    along_x = lambda other: spot(z, other, y)
    across = spot(z, x, 1 - y)
    core_mate = (feat, pair + 1 - 2 * lax.rem(pair, 2))
    chip_mate = (feat, lax.rem(pair + 2, 4))

    barrier = pltpu.get_barrier_semaphore()
    greeted = (
        along_z(near_z(1)), along_z(near_z(-1)), along_x(near_x(1)), along_x(near_x(-1)),
        across, core_mate, chip_mate,
    )
    for device in greeted:
        pl.semaphore_signal(barrier, inc=1, device_id=device, device_id_type=MESH)

    for slot in range(1, 4):

        @pl.when(pair < slot)
        def _():
            cat[:, :, slot * width : (slot + 1) * width] = jnp.zeros((NZ, BLOCK, width), BF16)

    pl.semaphore_wait(barrier, len(greeted))
    plan = Plan()

    low_chip, low_core = pair < 2, lax.rem(pair, 2) == 0
    relayed = lax.rem(pair, 2)

    def piece(slot, k):
        return cat.at[order[k], :, pl.ds(pl.multiple_of(slot * width, width), width)]

    def send_piece(kind, slot, k, device):
        return pltpu.make_async_remote_copy(
            src_ref=piece(slot, k), dst_ref=piece(slot, k),
            send_sem=pair_send.at[kind, k], recv_sem=pair_recv.at[slot, k],
            device_id=device, device_id_type=MESH,
        )

    def await_piece(slot, k):
        send_piece(0, slot, k, core_mate).wait_recv()

    def chosen_of(k):
        tokens = pl.ds(pl.multiple_of(order[k] * BLOCK, BLOCK), BLOCK)
        local = act_ref[:, tokens] - feat * width
        word = lax.shift_right_arithmetic(local, 5)
        bit = lax.shift_left(jnp.int32(1), local & 31)
        words = [
            jnp.sum(jnp.where(word == w, bit, 0), axis=0, keepdims=True)
            for w in range(width // 32)
        ]
        spread = jnp.concatenate([jnp.broadcast_to(w, (32, BLOCK)) for w in words], axis=0)
        place = lax.broadcasted_iota(jnp.int32, (width, BLOCK), 0) & 31
        return (lax.shift_right_logical(spread, place) & 1).astype(F32).T

    def values(ks):
        for k in ks:
            resid_copies[k].wait()
        if ks[0] == 0:
            enc_copy.wait()
        rows = jnp.concatenate([resid[k] for k in ks], axis=0)
        pre = jnp.dot(rows, enc[...], preferred_element_type=F32) + enc_bias_ref[...]
        for n, k in enumerate(ks):
            kept = jnp.maximum(pre[n * BLOCK : (n + 1) * BLOCK], 0.0)
            piece(pair, k)[...] = jnp.where(chosen_of(k) > 0.5, kept, 0.0).astype(BF16)

        @pl.when(low_chip)
        def _():
            for k in ks:
                send_piece(0, pair, k, chip_mate).start()

        @pl.when(low_core)
        def _():
            for k in ks:
                send_piece(1, pair, k, core_mate).start()

    def relay(ks):
        @pl.when(jnp.logical_not(low_chip))
        def _():
            for k in ks:
                await_piece(relayed, k)
                send_piece(2, relayed, k, core_mate).start()

    def collect(ks):
        @pl.when(jnp.logical_not(low_chip))
        def _():
            for k in ks:
                await_piece(1 - relayed, k)

        for holder, slot in ((1, 0), (3, 2)):

            @pl.when(pair == holder)
            def _():
                for k in ks:
                    await_piece(slot, k)

    def decode(ks, c):
        if c == 0:
            if ks[0] == 0:
                dec_copy.wait()
            collect(ks)
        step = 512

        @pl.loop(2 * c, 2 * c + 2)
        def _(i):
            cols = pl.ds(pl.multiple_of(i * step, step), step)
            rows = jnp.concatenate([cat[order[k]] for k in ks], axis=0)
            product = jnp.dot(rows, dec[:, cols], preferred_element_type=F32).astype(BF16)
            for n, k in enumerate(ks):
                part[order[k], :, cols] = product[n * BLOCK : (n + 1) * BLOCK]

    decoded = [{}, {}]
    before = ()
    for ks in GROUPS:
        name = ("v", ks)
        before = [
            plan.add(
                lambda ks=ks: values(ks), 0.35 + 0.45 * len(ks),
                after=before, sends=[(name, "mate", 65536 * len(ks))], bias=100.0,
            )
        ]
        plan.add(lambda ks=ks: relay(ks), 0.1, needs=[name], sends=[(("r", ks), "core", 3000)], bias=200.0)
        last = ()
        for c in range(2):
            last = [
                plan.add(
                    lambda ks=ks, c=c: decode(ks, c), 0.35 + 0.3 * len(ks),
                    after=last, needs=[("r", ks)] if c == 0 else [], bias=40.0 - 40.0 * c,
                )
            ]
            for k in ks:
                decoded[c][k] = last[0]

    def turn(k):
        turned[:, pl.ds(pl.multiple_of(order[k] * BLOCK, BLOCK), BLOCK)] = cat[order[k]].T

    turns = [plan.add(lambda k=k: turn(k), 0.35, after=[decoded[1][k]]) for k in range(NZ)]

    def rows16(index, half):
        return pl.ds(pl.multiple_of(index * 32 + half * 16, 16), 16)

    def rows_of(xx, half):
        return rows16(xx, y if half == 0 else 1 - y)

    def over_y(which, src, dst):
        return pltpu.make_async_remote_copy(
            src_ref=src, dst_ref=dst, send_sem=y_send.at[which], recv_sem=y_recv.at[which],
            device_id=across, device_id_type=MESH,
        )

    rings, y_copies, arrived = [], [], {}
    base = 0
    for c, (wide_a, wide_b) in enumerate(SETS):
        bias = 40.0 - 40.0 * c
        at_a, at_b = slice(base, base + wide_a), slice(base + wide_a, base + wide_a + wide_b)
        cols_a, cols_b = pl.ds(base, wide_a), pl.ds(base + wide_a, wide_b)
        base += wide_a + wide_b

        az = Reduce(
            ("az", c), NZ, z, along_z, "z", 128 * wide_a, s_az.at[c], r_az.at[c],
            own=lambda i, h, cols=cols_a: part.at[i, pl.ds(h * 64, 64), cols], held=held_az[c],
        )
        ax = Reduce(
            ("ax", c), NX, x, along_x, "x", 32 * wide_a, s_ax.at[c], r_ax.at[c],
            own=lambda i, h, mid=mid_a[c]: mid.at[rows16(i, h)], held=held_ax[c],
        )
        bx = [
            Reduce(
                ("bx", c, k), NX, x, along_x, "x", 32 * wide_b, s_bx.at[c, k], r_bx.at[c, k],
                own=lambda i, h, o=o, cols=cols_b: part.at[o, rows16(i, h), cols], held=held_bx[c].at[k],
            )
            for k, o in enumerate(order)
        ]
        bz = Reduce(
            ("bz", c), NZ, z, along_z, "z", 32 * wide_b, s_bz.at[c], r_bz.at[c],
            own=lambda i, h, mid=mid_b[c]: mid.at[i, pl.ds(h * 16, 16)], held=held_bz[c],
        )
        rings += [az, ax, bz, *bx]

        def keep_a(half, value, mid=mid_a[c]):
            mid[half * 64 : half * 64 + 64] = value.astype(BF16)

        def keep_end(which):
            def keep(half, value):
                end[which][half] = value
                give[which][half] = value.astype(BF16)

            return keep

        def block_ready(by, half, c=c):
            return [decoded[c][0 if by == -4 else place_of[by]]]

        summed_a = az.plan(plan, block_ready, keep_a, 0.12, bias)
        ended_a = ax.plan(plan, lambda by, half: summed_a, keep_end(2 * c), 0.06, bias)
        summed_b = []
        for k in range(NZ):

            def keep_b(half, value, o=order[k], mid=mid_b[c]):
                mid[o, half * 16 : half * 16 + 16] = value.astype(BF16)

            summed_b.append(bx[k].plan(plan, lambda by, half, k=k: [decoded[c][k]], keep_b, 0.07, bias))
        ended_b = bz.plan(
            plan, lambda by, half: [summed_b[0 if by == -4 else place_of[by]][half]], keep_end(2 * c + 1), 0.07, bias
        )

        gax = Gather(
            ("gax", c), NX, x, along_x, "x", 32 * wide_a, g_ax.at[c], h_ax.at[c],
            view=lambda i, h, cols=cols_a: full.at[z, rows_of(i, h), cols],
        )
        gbz = Gather(
            ("gbz", c), NZ, z, along_z, "z", 32 * wide_b, g_bz.at[c], h_bz.at[c],
            view=lambda i, h, cols=cols_b: full.at[i, rows_of(x, h), cols],
        )
        gaz = {
            by: Gather(
                ("gaz", c, by), NZ, z, along_z, "z", 32 * wide_a, g_az.at[c, n], h_az.at[c, n],
                view=lambda i, h, xx=near_x(by), cols=cols_a: full.at[i, rows_of(xx, h), cols],
            )
            for n, by in enumerate((0, -1, 1, 2))
        }
        gbx = {
            by: Gather(
                ("gbx", c, by), NX, x, along_x, "x", 32 * wide_b, g_bx.at[c, n], h_bx.at[c, n],
                view=lambda i, h, zz=near_z(by), cols=cols_b: full.at[zz, rows_of(i, h), cols],
            )
            for n, by in enumerate((0, -1, 1, -2, 2, -3, 3, 4))
        }
        rings += [gax, gbz, *gaz.values(), *gbx.values()]

        for part_index, ended, cols, at, wide, first, then in (
            (0, ended_a, cols_a, at_a, wide_a, gax, gaz),
            (1, ended_b, cols_b, at_b, wide_b, gbz, gbx),
        ):
            which = 2 * c + part_index

            def cross(which=which):
                copy = over_y(which, give[which].at[1 - y], take[which])
                copy.start()
                y_copies.append(copy)

            crossed = plan.add(cross, 0.04, after=ended, sends=[(("y", which), "y", 32 * wide)], bias=bias)

            def settle(which=which, cols=cols, at=at, first=first, ring=then[0]):
                over_y(which, take[which], take[which]).wait_recv()
                rebuilt = end[which][y] + take[which][...].astype(F32)
                error = rebuilt + dec_bias_ref[:, at] - target_ref[:, at].astype(F32)
                block = full.at[z, rows_of(x, 0), cols]
                block[...] = error.astype(BF16)
                err_ref[:, at] = error
                copy = over_y(4 + which, block, block)
                copy.start()
                y_copies.append(copy)
                first.first(0)
                ring.first(0)

            settled = plan.add(
                settle, 0.25, after=[crossed], needs=[("y", which)],
                sends=[(("e", which), "y", 32 * wide), *first.first_messages(0), *then[0].first_messages(0)],
            )

            def greet(which=which, cols=cols, first=first, ring=then[0]):
                block = full.at[z, rows_of(x, 1), cols]
                over_y(4 + which, block, block).wait_recv()
                first.first(1)
                ring.first(1)

            greeted_y = plan.add(
                greet, 0.15, after=[settled], needs=[("e", which)],
                sends=[*first.first_messages(1), *then[0].first_messages(1)],
            )
            ends = [settled, greeted_y]
            if part_index == 0:
                ends += first.plan(plan, lambda by, then=then: then[2 if abs(by) == 2 else by])
            else:
                ends += first.plan(plan, lambda by, then=then: then[4 if abs(by) == 4 else by])
            for ring in then.values():
                ends += ring.plan(plan)
            arrived[which] = (at, ends)

    step = 256
    grad_copies = []
    for n in range(part.shape[2] // step):

        def grad(n=n):
            cols = slice(n * step, (n + 1) * step)
            rows = full[:, :, cols].reshape(-1, step)
            grads[:, cols] = jnp.dot(turned[...], rows, preferred_element_type=F32).astype(BF16)
            copy = pltpu.make_async_copy(
                grads.at[:, pl.ds(n * step, step)], grads_hbm.at[:, pl.ds(n * step, step)], store.at[n]
            )
            copy.start()
            grad_copies.append(copy)

        after = [*turns]
        for at, ends in arrived.values():
            if at.start < (n + 1) * step and at.stop > n * step:
                after += ends
        plan.add(grad, 0.75, after=after)

    plan.run()

    for ring in rings:
        ring.drain()
    for copy in y_copies:
        copy.wait_send()

    @pl.when(low_chip)
    def _():
        for k in range(NZ):
            send_piece(0, pair, k, chip_mate).wait_send()

    @pl.when(low_core)
    def _():
        for k in range(NZ):
            send_piece(1, pair, k, core_mate).wait_send()

    @pl.when(jnp.logical_not(low_chip))
    def _():
        for k in range(NZ):
            send_piece(2, relayed, k, core_mate).wait_send()

    for copy in grad_copies:
        copy.wait()


def step(active, resid, enc, enc_bias, dec, dec_bias, target):
    tokens, model = resid.shape
    width, stacked = enc.shape[1], dec.shape[0]
    dma, vmem = pltpu.SemaphoreType.DMA, pltpu.VMEM
    here, there = pl.BlockSpec(memory_space=pltpu.VMEM), pl.BlockSpec(memory_space=pl.ANY)
    long, short = (2, 2, NZ // 2), (2, 2, NX // 2)
    parts = [wide for pair in SETS for wide in pair]
    per_set = lambda shape: [dma((len(SETS), *shape))] * 2
    return pl.pallas_call(
        step_kernel,
        out_shape=(
            jax.ShapeDtypeStruct(target.shape, F32),
            jax.ShapeDtypeStruct((stacked, model), BF16),
        ),
        in_specs=[here, there, there, here, there, here, here],
        out_specs=(here, there),
        scratch_shapes=[
            vmem((NZ, BLOCK, model), BF16),
            vmem((model, width), BF16),
            vmem((stacked, model), BF16),
            vmem((NZ, BLOCK, stacked), BF16),
            vmem((NZ, BLOCK, model), BF16),
            vmem((NZ, BLOCK, model), BF16),
            vmem((stacked, tokens), BF16),
            vmem((stacked, model), BF16),
            [vmem((BLOCK, a), BF16) for a, _ in SETS],
            [vmem((NZ, 32, b), BF16) for _, b in SETS],
            [vmem((2, 16, wide), F32) for wide in parts],
            [vmem((2, 16, wide), BF16) for wide in parts],
            [vmem((16, wide), BF16) for wide in parts],
            [vmem((*long, 64, a), BF16) for a, _ in SETS],
            [vmem((*short, 16, a), BF16) for a, _ in SETS],
            [vmem((NZ, *short, 16, b), BF16) for _, b in SETS],
            [vmem((*long, 16, b), BF16) for _, b in SETS],
            dma((NZ + 2,)),
            dma((model // 256,)),
            dma((3, NZ)),
            dma((4, NZ)),
            *per_set(long), *per_set(short), *per_set((NZ, *short)), *per_set(long),
            *per_set(short), *per_set((4, *long)), *per_set(long), *per_set((NZ, *short)),
            dma((8,)),
            dma((8,)),
        ],
        compiler_params=pltpu.CompilerParams(
            collective_id=0, has_side_effects=True, vmem_limit_bytes=60 * 1024 * 1024
        ),
    )(active, resid, enc, enc_bias, dec, dec_bias, target)


def local(resid, enc_weight, enc_bias, active, dec_weight, dec_bias, target):
    layers, width, model = dec_weight.shape[1:]
    error, grads = step(
        active[0].T, resid[0], enc_weight[0], enc_bias,
        dec_weight[0].reshape(layers * width, model), dec_bias, target[0],
    )
    return error[None], grads.reshape(1, layers, width, model)


def solution(mesh):
    in_specs = (
        P("pair", None, None),
        P("pair", None, "feat"),
        P("pair", "feat"),
        P("pair", None, None),
        P("pair", None, "feat", None),
        P("pair", None),
        P("pair", "feat", None),
    )
    out_specs = (P("pair", "feat", None), P("pair", None, "feat", None))
    return jax.shard_map(local, mesh=mesh, in_specs=in_specs, out_specs=out_specs, check_vma=False)
```

```python
import jax
import jax.numpy as jnp
from jax import lax
from jax.experimental import pallas as pl
from jax.experimental.pallas import tpu as pltpu
from jax.sharding import PartitionSpec as P

MESH = pl.DeviceIdType.MESH
F32, BF16 = jnp.float32, jnp.bfloat16
NZ, NX, NY = 8, 4, 2
UP, DN = 0, 1


BLOCK = 128
SETS = ((384, 640), (512, 512))
GROUPS = ((0,), (1, 2), (3, 4), (5, 6), (7,))
DISTANCES = (4, 3, -3, 2, -2, 1, -1, 0)
LONG, SHORT = ((UP, 0), (DN, 1)), ((UP, 1), (DN, 0))
STREAMS = LONG + SHORT
WIRE, LATENCY = 42e3, 3.5


class Plan:
    def __init__(self):
        self.steps, self.sender = [], {}

    def add(self, run, took, after=(), needs=(), sends=(), bias=0.0):
        me = len(self.steps)
        self.steps.append((run, took, tuple(after), tuple(needs), tuple(sends), bias))
        for key, _, _ in sends:
            self.sender[key] = me
        return me

    def order(self):
        count = len(self.steps)
        follows = [[] for _ in range(count)]
        ahead = [0] * count
        size = {key: n for step in self.steps for key, _, n in step[4]}
        for me, (_, _, after, needs, _, _) in enumerate(self.steps):
            for other in after:
                follows[other].append((me, 0.0))
            for key in needs:
                follows[self.sender[key]].append((me, LATENCY + size[key] / WIRE))
            ahead[me] = len(after) + len(needs)
        level, left = [0.0] * count, ahead[:]
        queue = [me for me in range(count) if left[me] == 0]
        for me in queue:
            for other, _ in follows[me]:
                left[other] -= 1
                if left[other] == 0:
                    queue.append(other)
        for me in reversed(queue):
            level[me] = self.steps[me][1] + max((d + level[o] for o, d in follows[me]), default=0.0)
        now, free, landed, done, result = 0.0, {}, {}, [False] * count, []
        waiting = list(range(count))
        while waiting:
            best = None
            for me in waiting:
                _, _, after, needs, _, bias = self.steps[me]
                if all(done[o] for o in after) and all(key in landed for key in needs):
                    at = max([now] + [landed[key] for key in needs])
                    rank = (at > now, at if at > now else 0.0, -level[me] - bias, me)
                    if best is None or rank < best[0]:
                        best = (rank, me, at)
            _, me, at = best
            now = at + self.steps[me][1]
            for key, link, n in self.steps[me][4]:
                start = max(now, free.get(link, 0.0))
                free[link] = start + n / WIRE
                landed[key] = free[link] + LATENCY
            done[me] = True
            waiting.remove(me)
            result.append(me)
        self.length = now
        return result

    def run(self):
        for me in self.order():
            self.steps[me][0]()


class Ring:
    def __init__(self, name, size, index, device, link, nbytes, sends, recvs):
        self.name, self.size, self.index, self.device = name, size, index, device
        self.link, self.nbytes, self.sends, self.recvs = link, nbytes, sends, recvs
        self.far = size // 2
        self.started = []

    def at(self, offset):
        return lax.rem(self.index + offset + self.size, self.size)

    def copy(self, way, half, step, src, dst):
        toward = self.at(1 if way == UP else -1)
        return pltpu.make_async_remote_copy(
            src_ref=src,
            dst_ref=dst,
            send_sem=self.sends.at[way, half, step - 1],
            recv_sem=self.recvs.at[way, half, step - 1],
            device_id=self.device(toward),
            device_id_type=MESH,
        )

    def go(self, *what):
        copy = self.copy(*what)
        copy.start()
        self.started.append(copy)

    def drain(self):
        for copy in self.started:
            copy.wait_send()

    def reach(self, way, half):
        return self.far if way == half else self.far - 1

    def key(self, way, half, step):
        return (*self.name, way, half, step)

    def message(self, way, half, step):
        return (self.key(way, half, step), self.link + str(way), self.nbytes)


class Reduce(Ring):
    def __init__(self, *ring, own, held):
        super().__init__(*ring)
        self.own, self.held = own, held

    def slot(self, way, half, step):
        return self.held.at[way, half, step - 1]

    def first(self, way, half):
        far = self.reach(way, half)
        dest = self.at(far if way == UP else -far)
        self.go(way, half, far, self.own(dest, half), self.slot(way, half, far))

    def arrive(self, way, half, step):
        slot = self.slot(way, half, step)
        self.copy(way, half, step, slot, slot).wait_recv()
        return slot

    def pass_on(self, way, half, step):
        slot = self.arrive(way, half, step + 1)
        own = self.own(self.at(step if way == UP else -step), half)
        slot[...] = (slot[...].astype(F32) + own[...].astype(F32)).astype(BF16)
        self.go(way, half, step, slot, self.slot(way, half, step))

    def total(self, half):
        up = self.arrive(UP, half, 1)
        down = self.arrive(DN, half, 1)
        own = self.own(self.index, half)
        return own[...].astype(F32) + (up[...].astype(F32) + down[...].astype(F32))

    def plan(self, plan, ready, finish, took, bias):
        for way, half in STREAMS:
            sign = 1 if way == UP else -1
            far = self.reach(way, half)
            plan.add(
                lambda w=way, h=half: self.first(w, h), 0.04,
                after=ready(sign * far, half), sends=[self.message(way, half, far)], bias=bias,
            )
            for step in range(far - 1, 0, -1):
                plan.add(
                    lambda w=way, h=half, s=step: self.pass_on(w, h, s), took,
                    after=ready(sign * step, half), needs=[self.key(way, half, step + 1)],
                    sends=[self.message(way, half, step)], bias=bias,
                )
        return [
            plan.add(
                lambda h=half: finish(h, self.total(h)), 1.5 * took,
                after=ready(0, half), needs=[self.key(way, half, 1) for way in (UP, DN)], bias=bias,
            )
            for half in range(2)
        ]


class Gather(Ring):
    def __init__(self, *ring, view):
        super().__init__(*ring)
        self.view = view

    def first(self, half):
        for way in (UP, DN):
            block = self.view(self.index, half)
            self.go(way, half, 1, block, block)

    def first_messages(self, half):
        return [self.message(way, half, 1) for way in (UP, DN)]

    def arrive(self, way, half, step):
        block = self.view(self.at(-step if way == UP else step), half)
        self.copy(way, half, step, block, block).wait_recv()
        if step < self.reach(way, half):
            self.go(way, half, step + 1, block, block)

    def plan(self, plan, then=None):
        added = []
        for way, half in STREAMS:
            for step in range(1, self.reach(way, half) + 1):
                sends = [self.message(way, half, step + 1)] if step < self.reach(way, half) else []
                ring = then(-step if way == UP else step) if then else None
                if ring:
                    sends += ring.first_messages(half)

                def run(w=way, h=half, s=step, ring=ring):
                    self.arrive(w, h, s)
                    if ring:
                        ring.first(h)

                added.append(plan.add(run, 0.06 + 0.03 * len(sends), needs=[self.key(way, half, step)], sends=sends))
        return added


def step_kernel(
    act_ref, resid_hbm, enc_hbm, enc_bias_ref, dec_hbm, dec_bias_ref, target_ref,
    err_ref, grads_hbm, turned_hbm, late_hbm,
    resid, enc, dec, cat, part, full, turned, grads,
    mid_a, mid_b, end, give, take, held_az, held_ax, held_bx, held_bz,
    load, store, pair_send, pair_recv,
    s_az, r_az, s_ax, r_ax, s_bx, r_bx, s_bz, r_bz,
    g_ax, h_ax, g_az, h_az, g_bz, h_bz, g_bx, h_bx,
    y_send, y_recv,
):
    feat, pair = lax.axis_index("feat"), lax.axis_index("pair")
    z, x, y = feat // (NX * NY), lax.rem(feat // NY, NX), lax.rem(feat, NY)
    width = enc.shape[1]

    near_z = lambda by: lax.rem(z + by + NZ, NZ)
    near_x = lambda by: lax.rem(x + by + NX, NX)
    order = [near_z(by) for by in DISTANCES]
    place_of = {by: k for k, by in enumerate(DISTANCES)}

    enc_copy = pltpu.make_async_copy(enc_hbm, enc, load.at[NZ])
    dec_copy = pltpu.make_async_copy(dec_hbm, dec, load.at[NZ + 1])
    resid_copies = [
        pltpu.make_async_copy(
            resid_hbm.at[pl.ds(pl.multiple_of(o * BLOCK, BLOCK), BLOCK)], resid.at[k], load.at[k]
        )
        for k, o in enumerate(order)
    ]
    enc_copy.start()
    for copy in resid_copies[:3]:
        copy.start()
    dec_copy.start()
    for copy in resid_copies[3:]:
        copy.start()

    def spot(zz, xx, yy):
        return ((zz * NX + xx) * NY + yy, pair)

    along_z = lambda other: spot(other, x, y)
    along_x = lambda other: spot(z, other, y)
    across = spot(z, x, 1 - y)
    core_mate = (feat, pair + 1 - 2 * lax.rem(pair, 2))
    chip_mate = (feat, lax.rem(pair + 2, 4))

    barrier = pltpu.get_barrier_semaphore()
    greeted = (
        along_z(near_z(1)), along_z(near_z(-1)), along_x(near_x(1)), along_x(near_x(-1)),
        across, core_mate, chip_mate,
    )
    for device in greeted:
        pl.semaphore_signal(barrier, inc=1, device_id=device, device_id_type=MESH)

    for slot in range(1, 4):

        @pl.when(pair < slot)
        def _():
            cat[:, :, slot * width : (slot + 1) * width] = jnp.zeros((NZ, BLOCK, width), BF16)

    pl.semaphore_wait(barrier, len(greeted))
    plan = Plan()

    low_chip, low_core = pair < 2, lax.rem(pair, 2) == 0
    relayed = lax.rem(pair, 2)

    def piece(slot, k):
        return cat.at[order[k], :, pl.ds(pl.multiple_of(slot * width, width), width)]

    def send_piece(kind, slot, k, device):
        return pltpu.make_async_remote_copy(
            src_ref=piece(slot, k), dst_ref=piece(slot, k),
            send_sem=pair_send.at[kind, k], recv_sem=pair_recv.at[slot, k],
            device_id=device, device_id_type=MESH,
        )

    def await_piece(slot, k):
        send_piece(0, slot, k, core_mate).wait_recv()

    def chosen_of(k):
        tokens = pl.ds(pl.multiple_of(order[k] * BLOCK, BLOCK), BLOCK)
        local = act_ref[:, tokens] - feat * width
        word = lax.shift_right_arithmetic(local, 5)
        bit = lax.shift_left(jnp.int32(1), local & 31)
        words = [
            jnp.sum(jnp.where(word == w, bit, 0), axis=0, keepdims=True)
            for w in range(width // 32)
        ]
        spread = jnp.concatenate([jnp.broadcast_to(w, (32, BLOCK)) for w in words], axis=0)
        place = lax.broadcasted_iota(jnp.int32, (width, BLOCK), 0) & 31
        return (lax.shift_right_logical(spread, place) & 1).astype(F32).T

    def values(ks):
        for k in ks:
            resid_copies[k].wait()
        if ks[0] == 0:
            enc_copy.wait()
        rows = jnp.concatenate([resid[k] for k in ks], axis=0)
        pre = jnp.dot(rows, enc[...], preferred_element_type=F32) + enc_bias_ref[...]
        for n, k in enumerate(ks):
            kept = jnp.maximum(pre[n * BLOCK : (n + 1) * BLOCK], 0.0)
            piece(pair, k)[...] = jnp.where(chosen_of(k) > 0.5, kept, 0.0).astype(BF16)

        @pl.when(low_chip)
        def _():
            for k in ks:
                send_piece(0, pair, k, chip_mate).start()

        @pl.when(low_core)
        def _():
            for k in ks:
                send_piece(1, pair, k, core_mate).start()

    def relay(ks):
        @pl.when(jnp.logical_not(low_chip))
        def _():
            for k in ks:
                await_piece(relayed, k)
                send_piece(2, relayed, k, core_mate).start()

    def collect(ks):
        @pl.when(jnp.logical_not(low_chip))
        def _():
            for k in ks:
                await_piece(1 - relayed, k)

        for holder, slot in ((1, 0), (3, 2)):

            @pl.when(pair == holder)
            def _():
                for k in ks:
                    await_piece(slot, k)

    def decode(ks, c):
        if c == 0:
            if ks[0] == 0:
                dec_copy.wait()
            collect(ks)
        step = 512

        first = sum(map(sum, SETS[:c])) // step

        @pl.loop(first, first + sum(SETS[c]) // step)
        def _(i):
            cols = pl.ds(pl.multiple_of(i * step, step), step)
            rows = jnp.concatenate([cat[order[k]] for k in ks], axis=0)
            product = jnp.dot(rows, dec[:, cols], preferred_element_type=F32).astype(BF16)
            for n, k in enumerate(ks):
                part[order[k], :, cols] = product[n * BLOCK : (n + 1) * BLOCK]

    decoded = [{} for _ in SETS]
    before = ()
    for ks in GROUPS:
        name = ("v", ks)
        before = [
            plan.add(
                lambda ks=ks: values(ks), 0.35 + 0.45 * len(ks),
                after=before, sends=[(name, "mate", 65536 * len(ks))], bias=100.0,
            )
        ]
        plan.add(lambda ks=ks: relay(ks), 0.1, needs=[name], sends=[(("r", ks), "core", 3000)], bias=200.0)
        last = ()
        for c in range(len(SETS)):
            last = [
                plan.add(
                    lambda ks=ks, c=c: decode(ks, c), (0.35 + 0.3 * len(ks)) * sum(SETS[c]) / 1024,
                    after=last, needs=[("r", ks)] if c == 0 else [], bias=40.0 - 40.0 * c,
                )
            ]
            for k in ks:
                decoded[c][k] = last[0]

    def turn(k):
        turned[:, pl.ds(pl.multiple_of(order[k] * BLOCK, BLOCK), BLOCK)] = cat[order[k]].T

    turns = [plan.add(lambda k=k: turn(k), 0.35, after=[decoded[-1][k]]) for k in range(NZ)]

    def rows16(index, half):
        return pl.ds(pl.multiple_of(index * 32 + half * 16, 16), 16)

    def rows_of(xx, half):
        return rows16(xx, y if half == 0 else 1 - y)

    def over_y(which, src, dst):
        return pltpu.make_async_remote_copy(
            src_ref=src, dst_ref=dst, send_sem=y_send.at[which], recv_sem=y_recv.at[which],
            device_id=across, device_id_type=MESH,
        )

    rings, y_copies, arrived = [], [], {}
    base = 0
    for c, (wide_a, wide_b) in enumerate(SETS):
        bias = 40.0 - 40.0 * c
        at_a, at_b = slice(base, base + wide_a), slice(base + wide_a, base + wide_a + wide_b)
        cols_a, cols_b = pl.ds(base, wide_a), pl.ds(base + wide_a, wide_b)
        base += wide_a + wide_b

        az = Reduce(
            ("az", c), NZ, z, along_z, "z", 128 * wide_a, s_az.at[c], r_az.at[c],
            own=lambda i, h, cols=cols_a: part.at[i, pl.ds(h * 64, 64), cols], held=held_az[c],
        )
        ax = Reduce(
            ("ax", c), NX, x, along_x, "x", 32 * wide_a, s_ax.at[c], r_ax.at[c],
            own=lambda i, h, mid=mid_a[c]: mid.at[rows16(i, h)], held=held_ax[c],
        )
        bx = [
            Reduce(
                ("bx", c, k), NX, x, along_x, "x", 32 * wide_b, s_bx.at[c, k], r_bx.at[c, k],
                own=lambda i, h, o=o, cols=cols_b: part.at[o, rows16(i, h), cols], held=held_bx[c].at[k],
            )
            for k, o in enumerate(order)
        ]
        bz = Reduce(
            ("bz", c), NZ, z, along_z, "z", 32 * wide_b, s_bz.at[c], r_bz.at[c],
            own=lambda i, h, mid=mid_b[c]: mid.at[i, pl.ds(h * 16, 16)], held=held_bz[c],
        )
        rings += [az, ax, bz, *bx]

        def keep_a(half, value, mid=mid_a[c]):
            mid[half * 64 : half * 64 + 64] = value.astype(BF16)

        def keep_end(which):
            def keep(half, value):
                end[which][half] = value
                give[which][half] = value.astype(BF16)

            return keep

        def block_ready(by, half, c=c):
            return [decoded[c][0 if by == -4 else place_of[by]]]

        summed_a = az.plan(plan, block_ready, keep_a, 0.12, bias)
        ended_a = ax.plan(plan, lambda by, half: summed_a, keep_end(2 * c), 0.06, bias)
        summed_b = []
        for k in range(NZ):

            def keep_b(half, value, o=order[k], mid=mid_b[c]):
                mid[o, half * 16 : half * 16 + 16] = value.astype(BF16)

            summed_b.append(bx[k].plan(plan, lambda by, half, k=k: [decoded[c][k]], keep_b, 0.07, bias))
        ended_b = bz.plan(
            plan, lambda by, half: [summed_b[0 if by == -4 else place_of[by]][half]], keep_end(2 * c + 1), 0.07, bias
        )

        gax = Gather(
            ("gax", c), NX, x, along_x, "x", 32 * wide_a, g_ax.at[c], h_ax.at[c],
            view=lambda i, h, cols=cols_a: full.at[z, rows_of(i, h), cols],
        )
        gbz = Gather(
            ("gbz", c), NZ, z, along_z, "z", 32 * wide_b, g_bz.at[c], h_bz.at[c],
            view=lambda i, h, cols=cols_b: full.at[i, rows_of(x, h), cols],
        )
        gaz = {
            by: Gather(
                ("gaz", c, by), NZ, z, along_z, "z", 32 * wide_a, g_az.at[c, n], h_az.at[c, n],
                view=lambda i, h, xx=near_x(by), cols=cols_a: full.at[i, rows_of(xx, h), cols],
            )
            for n, by in enumerate((0, -1, 1, 2))
        }
        gbx = {
            by: Gather(
                ("gbx", c, by), NX, x, along_x, "x", 32 * wide_b, g_bx.at[c, n], h_bx.at[c, n],
                view=lambda i, h, zz=near_z(by), cols=cols_b: full.at[zz, rows_of(i, h), cols],
            )
            for n, by in enumerate((0, -1, 1, -2, 2, -3, 3, 4))
        }
        rings += [gax, gbz, *gaz.values(), *gbx.values()]

        for part_index, ended, cols, at, wide, first, then in (
            (0, ended_a, cols_a, at_a, wide_a, gax, gaz),
            (1, ended_b, cols_b, at_b, wide_b, gbz, gbx),
        ):
            which = 2 * c + part_index

            def cross(which=which):
                copy = over_y(which, give[which].at[1 - y], take[which])
                copy.start()
                y_copies.append(copy)

            crossed = plan.add(cross, 0.04, after=ended, sends=[(("y", which), "y", 32 * wide)], bias=bias)

            def settle(which=which, cols=cols, at=at, first=first, ring=then[0]):
                over_y(which, take[which], take[which]).wait_recv()
                rebuilt = end[which][y] + take[which][...].astype(F32)
                error = rebuilt + dec_bias_ref[:, at] - target_ref[:, at].astype(F32)
                block = full.at[z, rows_of(x, 0), cols]
                block[...] = error.astype(BF16)
                err_ref[:, at] = error
                copy = over_y(2 * len(SETS) + which, block, block)
                copy.start()
                y_copies.append(copy)
                first.first(0)
                ring.first(0)

            settled = plan.add(
                settle, 0.25, after=[crossed], needs=[("y", which)],
                sends=[(("e", which), "y", 32 * wide), *first.first_messages(0), *then[0].first_messages(0)],
            )

            def greet(which=which, cols=cols, first=first, ring=then[0]):
                block = full.at[z, rows_of(x, 1), cols]
                over_y(2 * len(SETS) + which, block, block).wait_recv()
                first.first(1)
                ring.first(1)

            greeted_y = plan.add(
                greet, 0.15, after=[settled], needs=[("e", which)],
                sends=[*first.first_messages(1), *then[0].first_messages(1)],
            )
            ends = [settled, greeted_y]
            if part_index == 0:
                ends += first.plan(plan, lambda by, then=then: then[2 if abs(by) == 2 else by])
            else:
                ends += first.plan(plan, lambda by, then=then: then[4 if abs(by) == 4 else by])
            for ring in then.values():
                ends += ring.plan(plan)
            arrived[which] = (at, ends)

    step = 256
    early = sum(SETS[0])
    copies_out = []

    def put(src, dst):
        copy = pltpu.make_async_copy(src, dst, store.at[len(copies_out)])
        copy.start()
        copies_out.append(copy)

    plan.add(lambda: put(turned, turned_hbm), 0.05, after=turns)
    for n in range(early // step):

        def grad(n=n):
            cols = slice(n * step, (n + 1) * step)
            rows = full[:, :, cols].reshape(-1, step)
            grads[:, cols] = jnp.dot(turned[...], rows, preferred_element_type=F32).astype(BF16)
            put(grads.at[:, pl.ds(n * step, step)], grads_hbm.at[:, pl.ds(n * step, step)])

        after = [*turns]
        for at, ends in arrived.values():
            if at.start < (n + 1) * step and at.stop > n * step:
                after += ends
        plan.add(grad, 0.75, after=after)
    for at, ends in arrived.values():
        if at.start >= early:
            wide = at.stop - at.start
            plan.add(
                lambda at=at, wide=wide: put(
                    full.at[:, :, pl.ds(at.start, wide)], late_hbm.at[:, :, pl.ds(at.start - early, wide)]
                ),
                0.05, after=ends,
            )

    plan.run()

    for ring in rings:
        ring.drain()
    for copy in y_copies:
        copy.wait_send()

    @pl.when(low_chip)
    def _():
        for k in range(NZ):
            send_piece(0, pair, k, chip_mate).wait_send()

    @pl.when(low_core)
    def _():
        for k in range(NZ):
            send_piece(1, pair, k, core_mate).wait_send()

    @pl.when(jnp.logical_not(low_chip))
    def _():
        for k in range(NZ):
            send_piece(2, relayed, k, core_mate).wait_send()

    for copy in copies_out:
        copy.wait()


def step(active, resid, enc, enc_bias, dec, dec_bias, target):
    tokens, model = resid.shape
    width, stacked = enc.shape[1], dec.shape[0]
    dma, vmem = pltpu.SemaphoreType.DMA, pltpu.VMEM
    here, there = pl.BlockSpec(memory_space=pltpu.VMEM), pl.BlockSpec(memory_space=pl.ANY)
    long, short = (2, 2, NZ // 2), (2, 2, NX // 2)
    parts = [wide for pair in SETS for wide in pair]
    per_set = lambda shape: [dma((len(SETS), *shape))] * 2
    return pl.pallas_call(
        step_kernel,
        out_shape=(
            jax.ShapeDtypeStruct(target.shape, F32),
            jax.ShapeDtypeStruct((stacked, sum(SETS[0])), BF16),
            jax.ShapeDtypeStruct((stacked, tokens), BF16),
            jax.ShapeDtypeStruct((NZ, BLOCK, model - sum(SETS[0])), BF16),
        ),
        in_specs=[here, there, there, here, there, here, here],
        out_specs=(here, there, there, there),
        scratch_shapes=[
            vmem((NZ, BLOCK, model), BF16),
            vmem((model, width), BF16),
            vmem((stacked, model), BF16),
            vmem((NZ, BLOCK, stacked), BF16),
            vmem((NZ, BLOCK, model), BF16),
            vmem((NZ, BLOCK, model), BF16),
            vmem((stacked, tokens), BF16),
            vmem((stacked, sum(SETS[0])), BF16),
            [vmem((BLOCK, a), BF16) for a, _ in SETS],
            [vmem((NZ, 32, b), BF16) for _, b in SETS],
            [vmem((2, 16, wide), F32) for wide in parts],
            [vmem((2, 16, wide), BF16) for wide in parts],
            [vmem((16, wide), BF16) for wide in parts],
            [vmem((*long, 64, a), BF16) for a, _ in SETS],
            [vmem((*short, 16, a), BF16) for a, _ in SETS],
            [vmem((NZ, *short, 16, b), BF16) for _, b in SETS],
            [vmem((*long, 16, b), BF16) for _, b in SETS],
            dma((NZ + 2,)),
            dma((sum(SETS[0]) // 256 + 3,)),
            dma((3, NZ)),
            dma((4, NZ)),
            *per_set(long), *per_set(short), *per_set((NZ, *short)), *per_set(long),
            *per_set(short), *per_set((4, *long)), *per_set(long), *per_set((NZ, *short)),
            dma((4 * len(SETS),)),
            dma((4 * len(SETS),)),
        ],
        compiler_params=pltpu.CompilerParams(
            collective_id=0, has_side_effects=True, vmem_limit_bytes=60 * 1024 * 1024
        ),
    )(active, resid, enc, enc_bias, dec, dec_bias, target)


def finish_kernel(turned_ref, late_ref, early_ref, err_ref, out_ref, err_out_ref):
    block = pl.program_id(0)

    @pl.when(block == 0)
    def _():
        err_out_ref[...] = err_ref[...]

    @pl.when(block < 2)
    def _():
        product = jnp.dot(turned_ref[...], late_ref[...], preferred_element_type=F32)
        out_ref[...] = product.astype(BF16).reshape(out_ref.shape)

    @pl.when(block >= 2)
    def _():
        out_ref[...] = early_ref[...].reshape(out_ref.shape)


def finish(turned, late, early, error, layers):
    stacked, tokens = turned.shape
    block = 512
    model = late.shape[1] + early.shape[1]
    whole = lambda shape: pl.BlockSpec(shape, lambda i: (0, 0))
    return pl.pallas_call(
        finish_kernel,
        grid=(model // block,),
        out_shape=(
            jax.ShapeDtypeStruct((layers, stacked // layers, model), BF16),
            jax.ShapeDtypeStruct(error.shape, F32),
        ),
        in_specs=[
            whole((stacked, tokens)),
            pl.BlockSpec((tokens, block), lambda i: (0, jnp.minimum(i, 1))),
            pl.BlockSpec((stacked, block), lambda i: (0, jnp.maximum(i - 2, 0))),
            whole(error.shape),
        ],
        out_specs=(
            pl.BlockSpec((layers, stacked // layers, block), lambda i: (0, 0, lax.rem(i + 2, 4))),
            whole(error.shape),
        ),
        compiler_params=pltpu.CompilerParams(vmem_limit_bytes=60 * 1024 * 1024),
    )(turned, late, early, error)


def local(resid, enc_weight, enc_bias, active, dec_weight, dec_bias, target):
    layers, width, model = dec_weight.shape[1:]
    tokens = resid.shape[1]
    error, early, turned, late = step(
        active[0].T, resid[0], enc_weight[0], enc_bias,
        dec_weight[0].reshape(layers * width, model), dec_bias, target[0],
    )
    grads, error = finish(turned, late.reshape(tokens, -1), early, error, layers)
    return error[None], grads[None]


def solution(mesh):
    in_specs = (
        P("pair", None, None),
        P("pair", None, "feat"),
        P("pair", "feat"),
        P("pair", None, None),
        P("pair", None, "feat", None),
        P("pair", None),
        P("pair", "feat", None),
    )
    out_specs = (P("pair", "feat", None), P("pair", None, "feat", None))
    return jax.shard_map(local, mesh=mesh, in_specs=in_specs, out_specs=out_specs, check_vma=False)
```

```python
import jax
import jax.numpy as jnp
from jax import lax
from jax.experimental import pallas as pl
from jax.experimental.pallas import tpu as pltpu
from jax.sharding import PartitionSpec as P

MESH = pl.DeviceIdType.MESH
F32, BF16 = jnp.float32, jnp.bfloat16
NZ, NX, NY = 8, 4, 2
UP, DN = 0, 1


BLOCK = 128
SETS = ((384, 640), (512, 512))
GROUPS = ((0,), (1, 2), (3, 4), (5, 6), (7,))
DISTANCES = (4, 3, -3, 2, -2, 1, -1, 0)
LONG, SHORT = ((UP, 0), (DN, 1)), ((UP, 1), (DN, 0))
STREAMS = LONG + SHORT
WIRE, LATENCY = 42e3, 2.6


class Plan:
    def __init__(self):
        self.steps, self.sender = [], {}

    def add(self, run, took, after=(), needs=(), sends=(), bias=0.0):
        me = len(self.steps)
        self.steps.append((run, took, tuple(after), tuple(needs), tuple(sends), bias))
        for key, _, _ in sends:
            self.sender[key] = me
        return me

    def order(self):
        count = len(self.steps)
        follows = [[] for _ in range(count)]
        ahead = [0] * count
        size = {key: n for step in self.steps for key, _, n in step[4]}
        for me, (_, _, after, needs, _, _) in enumerate(self.steps):
            for other in after:
                follows[other].append((me, 0.0))
            for key in needs:
                follows[self.sender[key]].append((me, LATENCY + size[key] / WIRE))
            ahead[me] = len(after) + len(needs)
        level, left = [0.0] * count, ahead[:]
        queue = [me for me in range(count) if left[me] == 0]
        for me in queue:
            for other, _ in follows[me]:
                left[other] -= 1
                if left[other] == 0:
                    queue.append(other)
        for me in reversed(queue):
            level[me] = self.steps[me][1] + max((d + level[o] for o, d in follows[me]), default=0.0)
        now, free, landed, done, result = 0.0, {}, {}, [False] * count, []
        waiting = list(range(count))
        while waiting:
            best = None
            for me in waiting:
                _, _, after, needs, _, bias = self.steps[me]
                if all(done[o] for o in after) and all(key in landed for key in needs):
                    at = max([now] + [landed[key] for key in needs])
                    rank = (at > now, at if at > now else 0.0, -level[me] - bias, me)
                    if best is None or rank < best[0]:
                        best = (rank, me, at)
            _, me, at = best
            now = at + self.steps[me][1]
            for key, link, n in self.steps[me][4]:
                start = max(now, free.get(link, 0.0))
                free[link] = start + n / WIRE
                landed[key] = free[link] + LATENCY
            done[me] = True
            waiting.remove(me)
            result.append(me)
        self.length = now
        return result

    def run(self):
        for me in self.order():
            self.steps[me][0]()


class Ring:
    def __init__(self, name, size, index, device, link, nbytes, sends, recvs):
        self.name, self.size, self.index, self.device = name, size, index, device
        self.link, self.nbytes, self.sends, self.recvs = link, nbytes, sends, recvs
        self.far = size // 2
        self.started = []

    def at(self, offset):
        return lax.rem(self.index + offset + self.size, self.size)

    def copy(self, way, half, step, src, dst):
        toward = self.at(1 if way == UP else -1)
        return pltpu.make_async_remote_copy(
            src_ref=src,
            dst_ref=dst,
            send_sem=self.sends.at[way, half, step - 1],
            recv_sem=self.recvs.at[way, half, step - 1],
            device_id=self.device(toward),
            device_id_type=MESH,
        )

    def go(self, *what):
        copy = self.copy(*what)
        copy.start()
        self.started.append(copy)

    def drain(self):
        for copy in self.started:
            copy.wait_send()

    def reach(self, way, half):
        return self.far if way == half else self.far - 1

    def key(self, way, half, step):
        return (*self.name, way, half, step)

    def message(self, way, half, step):
        return (self.key(way, half, step), self.link + str(way), self.nbytes)


class Reduce(Ring):
    def __init__(self, *ring, own, held):
        super().__init__(*ring)
        self.own, self.held = own, held

    def slot(self, way, half, step):
        return self.held.at[way, half, step - 1]

    def first(self, way, half):
        far = self.reach(way, half)
        dest = self.at(far if way == UP else -far)
        self.go(way, half, far, self.own(dest, half), self.slot(way, half, far))

    def arrive(self, way, half, step):
        slot = self.slot(way, half, step)
        self.copy(way, half, step, slot, slot).wait_recv()
        return slot

    def pass_on(self, way, half, step):
        slot = self.arrive(way, half, step + 1)
        own = self.own(self.at(step if way == UP else -step), half)
        slot[...] = (slot[...].astype(F32) + own[...].astype(F32)).astype(BF16)
        self.go(way, half, step, slot, self.slot(way, half, step))

    def total(self, half):
        up = self.arrive(UP, half, 1)
        down = self.arrive(DN, half, 1)
        own = self.own(self.index, half)
        return own[...].astype(F32) + (up[...].astype(F32) + down[...].astype(F32))

    def plan(self, plan, ready, finish, took, bias):
        for way, half in STREAMS:
            sign = 1 if way == UP else -1
            far = self.reach(way, half)
            plan.add(
                lambda w=way, h=half: self.first(w, h), 0.04,
                after=ready(sign * far, half), sends=[self.message(way, half, far)], bias=bias,
            )
            for step in range(far - 1, 0, -1):
                plan.add(
                    lambda w=way, h=half, s=step: self.pass_on(w, h, s), took,
                    after=ready(sign * step, half), needs=[self.key(way, half, step + 1)],
                    sends=[self.message(way, half, step)], bias=bias,
                )
        return [
            plan.add(
                lambda h=half: finish(h, self.total(h)), 1.5 * took,
                after=ready(0, half), needs=[self.key(way, half, 1) for way in (UP, DN)], bias=bias,
            )
            for half in range(2)
        ]


class Gather(Ring):
    def __init__(self, *ring, view):
        super().__init__(*ring)
        self.view = view

    def first(self, half):
        for way in (UP, DN):
            block = self.view(self.index, half)
            self.go(way, half, 1, block, block)

    def first_messages(self, half):
        return [self.message(way, half, 1) for way in (UP, DN)]

    def arrive(self, way, half, step):
        block = self.view(self.at(-step if way == UP else step), half)
        self.copy(way, half, step, block, block).wait_recv()
        if step < self.reach(way, half):
            self.go(way, half, step + 1, block, block)

    def plan(self, plan, then=None):
        added = []
        for way, half in STREAMS:
            for step in range(1, self.reach(way, half) + 1):
                sends = [self.message(way, half, step + 1)] if step < self.reach(way, half) else []
                ring = then(-step if way == UP else step) if then else None
                if ring:
                    sends += ring.first_messages(half)

                def run(w=way, h=half, s=step, ring=ring):
                    self.arrive(w, h, s)
                    if ring:
                        ring.first(h)

                added.append(plan.add(run, 0.06 + 0.03 * len(sends), needs=[self.key(way, half, step)], sends=sends))
        return added


def step_kernel(
    act_ref, resid_hbm, enc_hbm, enc_bias_ref, dec_hbm, dec_bias_ref, target_ref,
    err_ref, grads_hbm, turned_hbm, late_hbm,
    resid, enc, dec, cat, part, full, turned, grads,
    mid_a, mid_b, end, give, take, held_az, held_ax, held_bx, held_bz,
    load, store, pair_send, pair_recv,
    s_az, r_az, s_ax, r_ax, s_bx, r_bx, s_bz, r_bz,
    g_ax, h_ax, g_az, h_az, g_bz, h_bz, g_bx, h_bx,
    y_send, y_recv,
):
    feat, pair = lax.axis_index("feat"), lax.axis_index("pair")
    z, x, y = feat // (NX * NY), lax.rem(feat // NY, NX), lax.rem(feat, NY)
    width = enc.shape[1]

    near_z = lambda by: lax.rem(z + by + NZ, NZ)
    near_x = lambda by: lax.rem(x + by + NX, NX)
    order = [near_z(by) for by in DISTANCES]
    place_of = {by: k for k, by in enumerate(DISTANCES)}

    enc_copy = pltpu.make_async_copy(enc_hbm, enc, load.at[NZ])
    dec_copy = pltpu.make_async_copy(dec_hbm, dec, load.at[NZ + 1])
    resid_copies = [
        pltpu.make_async_copy(
            resid_hbm.at[pl.ds(pl.multiple_of(o * BLOCK, BLOCK), BLOCK)], resid.at[k], load.at[k]
        )
        for k, o in enumerate(order)
    ]
    enc_copy.start()
    for copy in resid_copies[:3]:
        copy.start()
    dec_copy.start()
    for copy in resid_copies[3:]:
        copy.start()

    def spot(zz, xx, yy):
        return ((zz * NX + xx) * NY + yy, pair)

    along_z = lambda other: spot(other, x, y)
    along_x = lambda other: spot(z, other, y)
    across = spot(z, x, 1 - y)
    core_mate = (feat, pair + 1 - 2 * lax.rem(pair, 2))
    chip_mate = (feat, lax.rem(pair + 2, 4))

    barrier = pltpu.get_barrier_semaphore()
    greeted = (
        along_z(near_z(1)), along_z(near_z(-1)), along_x(near_x(1)), along_x(near_x(-1)),
        across, core_mate, chip_mate,
    )
    for device in greeted:
        pl.semaphore_signal(barrier, inc=1, device_id=device, device_id_type=MESH)

    for slot in range(1, 4):

        @pl.when(pair < slot)
        def _():
            cat[:, :, slot * width : (slot + 1) * width] = jnp.zeros((NZ, BLOCK, width), BF16)

    pl.semaphore_wait(barrier, len(greeted))
    plan = Plan()

    low_chip, low_core = pair < 2, lax.rem(pair, 2) == 0
    relayed = lax.rem(pair, 2)

    def piece(slot, k):
        return cat.at[order[k], :, pl.ds(pl.multiple_of(slot * width, width), width)]

    def send_piece(kind, slot, k, device):
        return pltpu.make_async_remote_copy(
            src_ref=piece(slot, k), dst_ref=piece(slot, k),
            send_sem=pair_send.at[kind, k], recv_sem=pair_recv.at[slot, k],
            device_id=device, device_id_type=MESH,
        )

    def await_piece(slot, k):
        send_piece(0, slot, k, core_mate).wait_recv()

    def chosen_of(k):
        tokens = pl.ds(pl.multiple_of(order[k] * BLOCK, BLOCK), BLOCK)
        local = act_ref[:, tokens] - feat * width
        word = lax.shift_right_arithmetic(local, 5)
        bit = lax.shift_left(jnp.int32(1), local & 31)
        words = [
            jnp.sum(jnp.where(word == w, bit, 0), axis=0, keepdims=True)
            for w in range(width // 32)
        ]
        spread = jnp.concatenate([jnp.broadcast_to(w, (32, BLOCK)) for w in words], axis=0)
        place = lax.broadcasted_iota(jnp.int32, (width, BLOCK), 0) & 31
        return (lax.shift_right_logical(spread, place) & 1).astype(F32).T

    def values(ks):
        for k in ks:
            resid_copies[k].wait()
        if ks[0] == 0:
            enc_copy.wait()
        rows = jnp.concatenate([resid[k] for k in ks], axis=0)
        pre = jnp.dot(rows, enc[...], preferred_element_type=F32) + enc_bias_ref[...]
        for n, k in enumerate(ks):
            kept = jnp.maximum(pre[n * BLOCK : (n + 1) * BLOCK], 0.0)
            piece(pair, k)[...] = jnp.where(chosen_of(k) > 0.5, kept, 0.0).astype(BF16)

        @pl.when(low_chip)
        def _():
            for k in ks:
                send_piece(0, pair, k, chip_mate).start()

        @pl.when(low_core)
        def _():
            for k in ks:
                send_piece(1, pair, k, core_mate).start()

    def relay(ks):
        @pl.when(jnp.logical_not(low_chip))
        def _():
            for k in ks:
                await_piece(relayed, k)
                send_piece(2, relayed, k, core_mate).start()

    def collect(ks):
        @pl.when(jnp.logical_not(low_chip))
        def _():
            for k in ks:
                await_piece(1 - relayed, k)

        for holder, slot in ((1, 0), (3, 2)):

            @pl.when(pair == holder)
            def _():
                for k in ks:
                    await_piece(slot, k)

    def decode(ks, c):
        if c == 0:
            if ks[0] == 0:
                dec_copy.wait()
            collect(ks)
        step = 512

        first = sum(map(sum, SETS[:c])) // step

        @pl.loop(first, first + sum(SETS[c]) // step)
        def _(i):
            cols = pl.ds(pl.multiple_of(i * step, step), step)
            rows = jnp.concatenate([cat[order[k]] for k in ks], axis=0)
            product = jnp.dot(rows, dec[:, cols], preferred_element_type=F32).astype(BF16)
            for n, k in enumerate(ks):
                part[order[k], :, cols] = product[n * BLOCK : (n + 1) * BLOCK]

    decoded = [{} for _ in SETS]
    before = ()
    for ks in GROUPS:
        name = ("v", ks)
        before = [
            plan.add(
                lambda ks=ks: values(ks), 0.35 + 0.45 * len(ks),
                after=before, sends=[(name, "mate", 65536 * len(ks))], bias=100.0,
            )
        ]
        plan.add(lambda ks=ks: relay(ks), 0.1, needs=[name], sends=[(("r", ks), "core", 3000)], bias=200.0)
        last = ()
        for c in range(len(SETS)):
            last = [
                plan.add(
                    lambda ks=ks, c=c: decode(ks, c), (0.35 + 0.3 * len(ks)) * sum(SETS[c]) / 1024,
                    after=last, needs=[("r", ks)] if c == 0 else [], bias=40.0 - 40.0 * c,
                )
            ]
            for k in ks:
                decoded[c][k] = last[0]

    def turn(k):
        turned[:, pl.ds(pl.multiple_of(order[k] * BLOCK, BLOCK), BLOCK)] = cat[order[k]].T

    turns = [plan.add(lambda k=k: turn(k), 0.35, after=[decoded[-1][k]]) for k in range(NZ)]

    def rows16(index, half):
        return pl.ds(pl.multiple_of(index * 32 + half * 16, 16), 16)

    def rows_of(xx, half):
        return rows16(xx, y if half == 0 else 1 - y)

    def over_y(which, src, dst):
        return pltpu.make_async_remote_copy(
            src_ref=src, dst_ref=dst, send_sem=y_send.at[which], recv_sem=y_recv.at[which],
            device_id=across, device_id_type=MESH,
        )

    rings, y_copies, arrived = [], [], {}
    base = 0
    for c, (wide_a, wide_b) in enumerate(SETS):
        bias = 40.0 - 40.0 * c
        at_a, at_b = slice(base, base + wide_a), slice(base + wide_a, base + wide_a + wide_b)
        cols_a, cols_b = pl.ds(base, wide_a), pl.ds(base + wide_a, wide_b)
        base += wide_a + wide_b

        az = Reduce(
            ("az", c), NZ, z, along_z, "z", 128 * wide_a, s_az.at[c], r_az.at[c],
            own=lambda i, h, cols=cols_a: part.at[i, pl.ds(h * 64, 64), cols], held=held_az[c],
        )
        ax = Reduce(
            ("ax", c), NX, x, along_x, "x", 32 * wide_a, s_ax.at[c], r_ax.at[c],
            own=lambda i, h, mid=mid_a[c]: mid.at[rows16(i, h)], held=held_ax[c],
        )
        bx = [
            Reduce(
                ("bx", c, k), NX, x, along_x, "x", 32 * wide_b, s_bx.at[c, k], r_bx.at[c, k],
                own=lambda i, h, o=o, cols=cols_b: part.at[o, rows16(i, h), cols], held=held_bx[c].at[k],
            )
            for k, o in enumerate(order)
        ]
        bz = Reduce(
            ("bz", c), NZ, z, along_z, "z", 32 * wide_b, s_bz.at[c], r_bz.at[c],
            own=lambda i, h, mid=mid_b[c]: mid.at[i, pl.ds(h * 16, 16)], held=held_bz[c],
        )
        rings += [az, ax, bz, *bx]

        def keep_a(half, value, mid=mid_a[c]):
            mid[half * 64 : half * 64 + 64] = value.astype(BF16)

        def keep_end(which):
            def keep(half, value):
                end[which][half] = value
                give[which][half] = value.astype(BF16)

            return keep

        def block_ready(by, half, c=c):
            return [decoded[c][0 if by == -4 else place_of[by]]]

        summed_a = az.plan(plan, block_ready, keep_a, 0.12, bias)
        ended_a = ax.plan(plan, lambda by, half: summed_a, keep_end(2 * c), 0.06, bias)
        summed_b = []
        for k in range(NZ):

            def keep_b(half, value, o=order[k], mid=mid_b[c]):
                mid[o, half * 16 : half * 16 + 16] = value.astype(BF16)

            summed_b.append(bx[k].plan(plan, lambda by, half, k=k: [decoded[c][k]], keep_b, 0.07, bias))
        ended_b = bz.plan(
            plan, lambda by, half: [summed_b[0 if by == -4 else place_of[by]][half]], keep_end(2 * c + 1), 0.07, bias
        )

        gax = Gather(
            ("gax", c), NX, x, along_x, "x", 32 * wide_a, g_ax.at[c], h_ax.at[c],
            view=lambda i, h, cols=cols_a: full.at[z, rows_of(i, h), cols],
        )
        gbz = Gather(
            ("gbz", c), NZ, z, along_z, "z", 32 * wide_b, g_bz.at[c], h_bz.at[c],
            view=lambda i, h, cols=cols_b: full.at[i, rows_of(x, h), cols],
        )
        gaz = {
            by: Gather(
                ("gaz", c, by), NZ, z, along_z, "z", 32 * wide_a, g_az.at[c, n], h_az.at[c, n],
                view=lambda i, h, xx=near_x(by), cols=cols_a: full.at[i, rows_of(xx, h), cols],
            )
            for n, by in enumerate((0, -1, 1, 2))
        }
        gbx = {
            by: Gather(
                ("gbx", c, by), NX, x, along_x, "x", 32 * wide_b, g_bx.at[c, n], h_bx.at[c, n],
                view=lambda i, h, zz=near_z(by), cols=cols_b: full.at[zz, rows_of(i, h), cols],
            )
            for n, by in enumerate((0, -1, 1, -2, 2, -3, 3, 4))
        }
        rings += [gax, gbz, *gaz.values(), *gbx.values()]

        for part_index, ended, cols, at, wide, first, then in (
            (0, ended_a, cols_a, at_a, wide_a, gax, gaz),
            (1, ended_b, cols_b, at_b, wide_b, gbz, gbx),
        ):
            which = 2 * c + part_index

            def cross(which=which):
                copy = over_y(which, give[which].at[1 - y], take[which])
                copy.start()
                y_copies.append(copy)

            crossed = plan.add(cross, 0.04, after=ended, sends=[(("y", which), "y", 32 * wide)], bias=bias)

            def settle(which=which, cols=cols, at=at, first=first, ring=then[0]):
                over_y(which, take[which], take[which]).wait_recv()
                rebuilt = end[which][y] + take[which][...].astype(F32)
                error = rebuilt + dec_bias_ref[:, at] - target_ref[:, at].astype(F32)
                block = full.at[z, rows_of(x, 0), cols]
                block[...] = error.astype(BF16)
                err_ref[:, at] = error
                copy = over_y(2 * len(SETS) + which, block, block)
                copy.start()
                y_copies.append(copy)
                first.first(0)
                ring.first(0)

            settled = plan.add(
                settle, 0.25, after=[crossed], needs=[("y", which)],
                sends=[(("e", which), "y", 32 * wide), *first.first_messages(0), *then[0].first_messages(0)],
            )

            def greet(which=which, cols=cols, first=first, ring=then[0]):
                block = full.at[z, rows_of(x, 1), cols]
                over_y(2 * len(SETS) + which, block, block).wait_recv()
                first.first(1)
                ring.first(1)

            greeted_y = plan.add(
                greet, 0.15, after=[settled], needs=[("e", which)],
                sends=[*first.first_messages(1), *then[0].first_messages(1)],
            )
            ends = [settled, greeted_y]
            if part_index == 0:
                ends += first.plan(plan, lambda by, then=then: then[2 if abs(by) == 2 else by])
            else:
                ends += first.plan(plan, lambda by, then=then: then[4 if abs(by) == 4 else by])
            for ring in then.values():
                ends += ring.plan(plan)
            arrived[which] = (at, ends)

    step = 256
    early = sum(SETS[0])
    copies_out = []

    def put(src, dst):
        copy = pltpu.make_async_copy(src, dst, store.at[len(copies_out)])
        copy.start()
        copies_out.append(copy)

    plan.add(lambda: put(turned, turned_hbm), 0.05, after=turns)
    for n in range(early // step):

        def grad(n=n):
            cols = slice(n * step, (n + 1) * step)
            rows = full[:, :, cols].reshape(-1, step)
            grads[:, cols] = jnp.dot(turned[...], rows, preferred_element_type=F32).astype(BF16)
            put(grads.at[:, pl.ds(n * step, step)], grads_hbm.at[:, pl.ds(n * step, step)])

        after = [*turns]
        for at, ends in arrived.values():
            if at.start < (n + 1) * step and at.stop > n * step:
                after += ends
        plan.add(grad, 0.75, after=after)
    for at, ends in arrived.values():
        if at.start >= early:
            wide = at.stop - at.start
            plan.add(
                lambda at=at, wide=wide: put(
                    full.at[:, :, pl.ds(at.start, wide)], late_hbm.at[:, :, pl.ds(at.start - early, wide)]
                ),
                0.05, after=ends,
            )

    plan.run()

    for ring in rings:
        ring.drain()
    for copy in y_copies:
        copy.wait_send()

    @pl.when(low_chip)
    def _():
        for k in range(NZ):
            send_piece(0, pair, k, chip_mate).wait_send()

    @pl.when(low_core)
    def _():
        for k in range(NZ):
            send_piece(1, pair, k, core_mate).wait_send()

    @pl.when(jnp.logical_not(low_chip))
    def _():
        for k in range(NZ):
            send_piece(2, relayed, k, core_mate).wait_send()

    for copy in copies_out:
        copy.wait()


def step(active, resid, enc, enc_bias, dec, dec_bias, target):
    tokens, model = resid.shape
    width, stacked = enc.shape[1], dec.shape[0]
    dma, vmem = pltpu.SemaphoreType.DMA, pltpu.VMEM
    here, there = pl.BlockSpec(memory_space=pltpu.VMEM), pl.BlockSpec(memory_space=pl.ANY)
    long, short = (2, 2, NZ // 2), (2, 2, NX // 2)
    parts = [wide for pair in SETS for wide in pair]
    per_set = lambda shape: [dma((len(SETS), *shape))] * 2
    return pl.pallas_call(
        step_kernel,
        out_shape=(
            jax.ShapeDtypeStruct(target.shape, F32),
            jax.ShapeDtypeStruct((stacked, sum(SETS[0])), BF16),
            jax.ShapeDtypeStruct((stacked, tokens), BF16),
            jax.ShapeDtypeStruct((NZ, BLOCK, model - sum(SETS[0])), BF16),
        ),
        in_specs=[here, there, there, here, there, here, here],
        out_specs=(here, there, there, there),
        scratch_shapes=[
            vmem((NZ, BLOCK, model), BF16),
            vmem((model, width), BF16),
            vmem((stacked, model), BF16),
            vmem((NZ, BLOCK, stacked), BF16),
            vmem((NZ, BLOCK, model), BF16),
            vmem((NZ, BLOCK, model), BF16),
            vmem((stacked, tokens), BF16),
            vmem((stacked, sum(SETS[0])), BF16),
            [vmem((BLOCK, a), BF16) for a, _ in SETS],
            [vmem((NZ, 32, b), BF16) for _, b in SETS],
            [vmem((2, 16, wide), F32) for wide in parts],
            [vmem((2, 16, wide), BF16) for wide in parts],
            [vmem((16, wide), BF16) for wide in parts],
            [vmem((*long, 64, a), BF16) for a, _ in SETS],
            [vmem((*short, 16, a), BF16) for a, _ in SETS],
            [vmem((NZ, *short, 16, b), BF16) for _, b in SETS],
            [vmem((*long, 16, b), BF16) for _, b in SETS],
            dma((NZ + 2,)),
            dma((sum(SETS[0]) // 256 + 3,)),
            dma((3, NZ)),
            dma((4, NZ)),
            *per_set(long), *per_set(short), *per_set((NZ, *short)), *per_set(long),
            *per_set(short), *per_set((4, *long)), *per_set(long), *per_set((NZ, *short)),
            dma((4 * len(SETS),)),
            dma((4 * len(SETS),)),
        ],
        compiler_params=pltpu.CompilerParams(
            collective_id=0, has_side_effects=True, vmem_limit_bytes=60 * 1024 * 1024
        ),
    )(active, resid, enc, enc_bias, dec, dec_bias, target)


def finish_kernel(turned_hbm, late_hbm, early_ref, err_ref, out_ref, err_out_ref, turned, late, load):
    block, step = pl.program_id(0), out_ref.shape[2]
    copies = [pltpu.make_async_copy(turned_hbm, turned, load.at[0])]
    for n in range(2):
        cols = pl.ds(n * step, step)
        copies.append(pltpu.make_async_copy(late_hbm.at[:, cols], late.at[:, cols], load.at[1 + n]))

    @pl.when(block == 0)
    def _():
        for copy in copies:
            copy.start()
        err_out_ref[...] = err_ref[...]

    @pl.when(block < 2)
    def _():
        out_ref[...] = early_ref[...].reshape(out_ref.shape)

    for n in range(2):

        @pl.when(block == 2 + n)
        def _():
            if n == 0:
                copies[0].wait()
            copies[1 + n].wait()
            rows = late[:, n * step : (n + 1) * step]
            product = jnp.dot(turned[...], rows, preferred_element_type=F32)
            out_ref[...] = product.astype(BF16).reshape(out_ref.shape)


def finish(turned, late, early, error, layers):
    stacked, tokens = turned.shape
    block = 512
    model = late.shape[1] + early.shape[1]
    there = pl.BlockSpec(memory_space=pl.ANY)
    whole = pl.BlockSpec(error.shape, lambda i: (0, 0))
    return pl.pallas_call(
        finish_kernel,
        grid=(model // block,),
        out_shape=(
            jax.ShapeDtypeStruct((layers, stacked // layers, model), BF16),
            jax.ShapeDtypeStruct(error.shape, F32),
        ),
        in_specs=[
            there,
            there,
            pl.BlockSpec((stacked, block), lambda i: (0, jnp.minimum(i, 1))),
            whole,
        ],
        out_specs=(
            pl.BlockSpec((layers, stacked // layers, block), lambda i: (0, 0, i)),
            whole,
        ),
        scratch_shapes=[
            pltpu.VMEM((stacked, tokens), BF16),
            pltpu.VMEM(late.shape, BF16),
            pltpu.SemaphoreType.DMA((3,)),
        ],
        compiler_params=pltpu.CompilerParams(vmem_limit_bytes=60 * 1024 * 1024),
    )(turned, late, early, error)


def local(resid, enc_weight, enc_bias, active, dec_weight, dec_bias, target):
    layers, width, model = dec_weight.shape[1:]
    tokens = resid.shape[1]
    error, early, turned, late = step(
        active[0].T, resid[0], enc_weight[0], enc_bias,
        dec_weight[0].reshape(layers * width, model), dec_bias, target[0],
    )
    grads, error = finish(turned, late.reshape(tokens, -1), early, error, layers)
    return error[None], grads[None]


def solution(mesh):
    in_specs = (
        P("pair", None, None),
        P("pair", None, "feat"),
        P("pair", "feat"),
        P("pair", None, None),
        P("pair", None, "feat", None),
        P("pair", None),
        P("pair", "feat", None),
    )
    out_specs = (P("pair", "feat", None), P("pair", None, "feat", None))
    return jax.shard_map(local, mesh=mesh, in_specs=in_specs, out_specs=out_specs, check_vma=False)
```
